256 devices in a mesh: event: 8 (over x, z_lo), cuts: 32 (over z_hi, y, core).
Axes of the slice: x: 4, y: 4, z: 8 (z_hi: 4, z_lo: 2; z = z_hi * 2 + z_lo), core: 2. Of those that a mesh axis runs over, the one named last changes fastest.
Arguments:
- forward_displacement: float32 [8, 557568], P('event', 'cuts'), may hold values from -6 to 6
- forward_velocity: float32 [8, 557568], P('event', 'cuts'), may hold values from -6 to 6
- adjoint_displacement: float32 [8, 557568], P('event', 'cuts'), may hold values from -6 to 6
- adjoint_velocity: float32 [8, 557568], P('event', 'cuts'), may hold values from -6 to 6
- inverse_mass: float32 [557568], P('cuts'), may hold values from 0.3 to 3
- shear_modulus: float32 [125, 8192], P(None, 'cuts'), may hold values from 0.5 to 4
- connectivity: int32 [125, 8192], P(None, 'cuts'), may hold values from 0 to 18512, as said below
- face_points: int32 [32, 1152], P('cuts'), may hold values from 0 to 1088, as said below
- element_count: int32 [32], P('cuts'), may hold values from 128 to 256, as said below
Outputs:
- forward_displacement_next: float32 [8, 557568], P('event', 'cuts')
- forward_velocity_next: float32 [8, 557568], P('event', 'cuts')
- adjoint_displacement_next: float32 [8, 557568], P('event', 'cuts')
- adjoint_velocity_next: float32 [8, 557568], P('event', 'cuts')
- shear_kernel: float32 [512, 1089], P('cuts')
The draws below stay inside these ranges and needn't reach their ends.
Inputs may be any that keep to these rules, and one draw needn't show every extreme that they name: `connectivity`: slot n of slice s is the element (ex, ey, ez) of a structured block of 4 x 8 x 8 elements, in an order drawn per slice; its point (i, j, k) has coordinates x = 4 ex + i, y = 4 ey + j, z = 4 ez + k and index x 1089 + y * 33 + z for x < 16; points with x = 16 lie on the next slice's first plane and have index 17424 + g, where g is their slot in the next slice's face list. `face_points`: row s lists in slots 0 to 1088 each point of slice s with x = 0 once; slots 1089 to 1151 hold 0. `element_count`: some slice has all 256 slots live in every draw.
All inputs are finite; a program needn't handle non-finite values.
Results may differ from the reference program's by a relative error of at most 0.0001.
Values sent between devices are 32-bit elements; how exact they have to be, the bound alone decides.
A program may use at most 128 MiB of HBM per device.

```python
import math
import jax
import jax.numpy as jnp
import numpy as np
from jax import lax

NGLL = 5
NGLL3 = 125
EY = 8
EZ = 8
NEL = 256
PXU = 16
PY = 33
PZ = 33
PYZ = 1089
NPTS = 17424
NBUF = 1152
SLICES = 32
EVENTS = 8


def slice_tables(key):
    face_key = jax.random.fold_in(key, 101)
    order_key = jax.random.fold_in(key, 202)

    def face_order(subkey):
        return jax.random.permutation(subkey, PYZ).astype(jnp.int32)

    def element_order(subkey):
        return jax.random.permutation(subkey, NEL).astype(jnp.int32)

    def slot_lookup(permuted):
        return jnp.zeros((PYZ,), jnp.int32).at[permuted].set(jnp.arange(PYZ, dtype=jnp.int32))
    face_perm = jax.vmap(face_order)(jax.random.split(face_key, SLICES))
    slot_of = jax.vmap(slot_lookup)(face_perm)
    orders = jax.vmap(element_order)(jax.random.split(order_key, SLICES))
    return (face_perm, slot_of, orders)


def draw_connectivity(key, part):
    face_perm, slot_of, orders = slice_tables(key)
    element = jnp.arange(NEL, dtype=jnp.int32)
    node = jnp.arange(NGLL3, dtype=jnp.int32)
    coord_x = (NGLL - 1) * (element // (EY * EZ))[None, :] + (node // (NGLL * NGLL))[:, None]
    coord_y = (NGLL - 1) * (element // EZ % EY)[None, :] + (node // NGLL % NGLL)[:, None]
    coord_z = (NGLL - 1) * (element % EZ)[None, :] + (node % NGLL)[:, None]
    column = coord_y * PZ + coord_z
    owned = coord_x * PYZ + column
    next_slots = jnp.roll(slot_of, -1, axis=0)
    ghost = NPTS + next_slots[:, column]
    point_table = jnp.where((coord_x < PXU)[None, :, :], owned[None, :, :], ghost)
    point_table = jnp.take_along_axis(point_table, orders[:, None, :], axis=2)
    return point_table.transpose(1, 0, 2).reshape(NGLL3, SLICES * NEL).astype(jnp.int32)


def draw_face_points(key, part):
    face_perm, slot_of, orders = slice_tables(key)
    return jnp.pad(face_perm, ((0, 0), (0, NBUF - PYZ))).astype(jnp.int32)


def draw_element_count(key, part):
    counts = jax.random.randint(jax.random.fold_in(key, 303), (SLICES,), NEL // 2, NEL + 1, dtype=jnp.int32)
    fullest = jax.random.randint(jax.random.fold_in(key, 404), (), 0, SLICES, dtype=jnp.int32)
    return counts.at[fullest].set(NEL).astype(jnp.int32)


def level_of(key, dims, cuts, least, high):
    factor_of, own = 1.0, jax.random.fold_in(key, 6)
    for position, blocks in cuts:
        steps = jnp.exp(jax.random.uniform(jax.random.fold_in(own, position), (blocks,), jnp.float32, least / len(cuts), high / len(cuts)))
        factor_of = factor_of * jnp.repeat(steps, dims[position] // blocks).reshape([-1 if axis == position else 1 for axis in range(len(dims))])
    return factor_of


def noise(rng, extent, width, reach, cuts=(), kind=jnp.bfloat16):
    entries = jax.random.normal(rng, extent, jnp.float32) * width
    if len(cuts) > 0:
        entries = level_of(rng, extent, cuts, -0.22, 0.18) * entries
    return jnp.clip(entries, min=-reach, max=reach).astype(kind)


def setup_inputs(seed: int = 0) -> dict:
    keys = jax.random.split(jax.random.key(seed), 10)
    forward_displacement = noise(keys[0], (EVENTS, SLICES * NPTS), 1.0, 6.0, ((0, 8), (1, 32)), jnp.float32)
    forward_velocity = noise(keys[1], (EVENTS, SLICES * NPTS), 1.0, 6.0, ((0, 8), (1, 32)), jnp.float32)
    adjoint_displacement = noise(keys[2], (EVENTS, SLICES * NPTS), 1.0, 6.0, ((0, 8), (1, 32)), jnp.float32)
    adjoint_velocity = noise(keys[3], (EVENTS, SLICES * NPTS), 1.0, 6.0, ((0, 8), (1, 32)), jnp.float32)
    inverse_mass = jnp.clip(jnp.exp(math.log(3.0) - 2.3025851 * jax.random.uniform(keys[4], (SLICES * NPTS,), jnp.float32) ** level_of(keys[4], (SLICES * NPTS,), ((0, 32),), -0.2, 0.2)), 0.3, 3.0)
    shear_modulus = jnp.clip(jnp.exp(math.log(4.0) - 2.0794415 * jax.random.uniform(keys[5], (NGLL3, SLICES * NEL), jnp.float32) ** level_of(keys[5], (NGLL3, SLICES * NEL), ((1, 32),), -0.2, 0.2)), 0.5, 4.0)
    connectivity = draw_connectivity(jax.random.fold_in(keys[9], 71), 0)
    face_points = draw_face_points(jax.random.fold_in(keys[9], 71), 0)
    element_count = draw_element_count(jax.random.fold_in(keys[9], 71), 0)
    return {"forward_displacement": forward_displacement, "forward_velocity": forward_velocity, "adjoint_displacement": adjoint_displacement, "adjoint_velocity": adjoint_velocity, "inverse_mass": inverse_mass, "shear_modulus": shear_modulus, "connectivity": connectivity, "face_points": face_points, "element_count": element_count}


time_step = 0.02
cross_sigma = 1.5
cross_reach = 4

def gll_tables():
    nodes = np.array([-1.0, -np.sqrt(3.0 / 7.0), 0.0, np.sqrt(3.0 / 7.0), 1.0])
    quad_weights = np.array([0.1, 49.0 / 90.0, 32.0 / 45.0, 49.0 / 90.0, 0.1])
    barycentric = np.array([1.0 / np.prod([nodes[node_row] - nodes[node_column] for node_column in range(5) if node_column != node_row]) for node_row in range(5)])
    derivative = np.zeros((5, 5))
    for node_row in range(5):
        for node_column in range(5):
            if node_column != node_row:
                derivative[node_row, node_column] = barycentric[node_column] / barycentric[node_row] / (nodes[node_row] - nodes[node_column])
        derivative[node_row, node_row] = -np.sum(derivative[node_row])
    weights_cube = (quad_weights[:, None, None] * quad_weights[None, :, None] * quad_weights[None, None, :]).reshape(125)
    return (jnp.asarray(derivative, dtype=jnp.float32), jnp.asarray(weights_cube, dtype=jnp.float32))

def gradients(cube, derivative):
    grad_x = jnp.einsum('il,ljkn->ijkn', derivative, cube, precision=lax.Precision.HIGHEST)
    grad_y = jnp.einsum('jl,ilkn->ijkn', derivative, cube, precision=lax.Precision.HIGHEST)
    grad_z = jnp.einsum('kl,ijln->ijkn', derivative, cube, precision=lax.Precision.HIGHEST)
    return (grad_x, grad_y, grad_z)

def stiffness(grads, flux_cube, derivative):
    term_x = jnp.einsum('li,ljkn->ijkn', derivative, flux_cube * grads[0], precision=lax.Precision.HIGHEST)
    term_y = jnp.einsum('lj,ilkn->ijkn', derivative, flux_cube * grads[1], precision=lax.Precision.HIGHEST)
    term_z = jnp.einsum('lk,ijln->ijkn', derivative, flux_cube * grads[2], precision=lax.Precision.HIGHEST)
    return -(term_x + term_y + term_z)

def slice_terms(forward_ext, adjoint_ext, connect_slice, flux_slice, derivative):
    elements = connect_slice.shape[1]
    forward_grads = gradients(forward_ext[connect_slice].reshape(NGLL, NGLL, NGLL, elements), derivative)
    adjoint_grads = gradients(adjoint_ext[connect_slice].reshape(NGLL, NGLL, NGLL, elements), derivative)
    flux_cube = flux_slice.reshape(NGLL, NGLL, NGLL, elements)
    point_ids = connect_slice.reshape(-1)
    total = NPTS + NBUF
    forward_force = jax.ops.segment_sum(stiffness(forward_grads, flux_cube, derivative).reshape(-1), point_ids, num_segments=total)
    adjoint_force = jax.ops.segment_sum(stiffness(adjoint_grads, flux_cube, derivative).reshape(-1), point_ids, num_segments=total)
    product = forward_grads[0] * adjoint_grads[0] + forward_grads[1] * adjoint_grads[1] + forward_grads[2] * adjoint_grads[2]
    kernel_ext = jax.ops.segment_sum((-flux_cube * product).reshape(-1), point_ids, num_segments=total)
    return (forward_force, adjoint_force, kernel_ext)

def along_weight(offset):
    sigma = PXU / 4.0
    return jnp.exp(-offset * offset / (2.0 * sigma * sigma))

def cross_matrix(count):
    point_index = jnp.arange(count, dtype=jnp.int32)
    offset = (point_index[:, None] - point_index[None, :]).astype(jnp.float32)
    kept = jnp.exp(-offset * offset / (2.0 * cross_sigma * cross_sigma)) * (jnp.abs(offset) <= cross_reach).astype(jnp.float32)
    return kept / lax.optimization_barrier(jnp.sum(kept, axis=1, keepdims=True))

def cross_table():
    return jnp.kron(cross_matrix(PY), cross_matrix(PZ))

def along_norm():
    offsets = jnp.arange(-PXU, PXU + 1, dtype=jnp.int32).astype(jnp.float32)
    return jnp.sum(along_weight(offsets))

def cycle_matrix():
    count_rows = SLICES * PXU
    row_index = jnp.arange(count_rows, dtype=jnp.int32)
    spread = (row_index[None, :] - row_index[:, None]) % count_rows
    spread = jnp.where(spread > count_rows // 2, spread - count_rows, spread)
    inside = (jnp.abs(spread) <= PXU).astype(jnp.float32)
    return along_weight(spread.astype(jnp.float32)) * inside / along_norm()

def add_faces(owned, indices, received):
    return owned.at[indices].add(received)

def reference(forward_displacement, forward_velocity, adjoint_displacement, adjoint_velocity, inverse_mass, shear_modulus, connectivity, face_points, element_count):
    derivative, weights_cube = gll_tables()
    slice_connect = connectivity.reshape(NGLL3, SLICES, NEL).transpose(1, 0, 2)
    slice_shear = shear_modulus.reshape(NGLL3, SLICES, NEL).transpose(1, 0, 2)
    active = (jnp.arange(NEL, dtype=jnp.int32)[None, :] < element_count[:, None]).astype(jnp.float32)
    slice_flux = weights_cube[None, :, None] * slice_shear * active[:, None, :]
    mass_rows = inverse_mass.reshape(SLICES, NPTS)

    def extend(points):
        face_values = jnp.take_along_axis(points, face_points, axis=1)
        return jnp.concatenate([points, jnp.roll(face_values, -1, axis=0)], axis=1)

    def finish(extended):
        received = jnp.roll(extended[:, NPTS:], 1, axis=0)
        return jax.vmap(add_faces)(extended[:, :NPTS], face_points, received)

    def one_event(fields):
        forward_now = fields[0].reshape(SLICES, NPTS)
        forward_speed = fields[1].reshape(SLICES, NPTS)
        adjoint_now = fields[2].reshape(SLICES, NPTS)
        adjoint_speed = fields[3].reshape(SLICES, NPTS)
        forward_force, adjoint_force, kernel_ext = jax.vmap(slice_terms, in_axes=(0, 0, 0, 0, None))(extend(forward_now), extend(adjoint_now), slice_connect, slice_flux, derivative)
        forward_force = finish(forward_force)
        adjoint_force = finish(adjoint_force)
        kernel_points = finish(kernel_ext)
        forward_speed_next = forward_speed - time_step * mass_rows * forward_force
        forward_now_next = forward_now - time_step * forward_speed_next
        adjoint_speed_next = adjoint_speed + time_step * mass_rows * adjoint_force
        adjoint_now_next = adjoint_now + time_step * adjoint_speed_next
        return (forward_now_next.reshape(-1), forward_speed_next.reshape(-1), adjoint_now_next.reshape(-1), adjoint_speed_next.reshape(-1), kernel_points)
    results = lax.map(one_event, (forward_displacement, forward_velocity, adjoint_displacement, adjoint_velocity))
    kernel_total = lax.optimization_barrier(jnp.sum(results[4], axis=0)).reshape(SLICES * PXU, PYZ)
    smoothed_along = jnp.dot(cycle_matrix(), kernel_total, precision=lax.Precision.HIGHEST)
    shear_kernel = jnp.dot(smoothed_along, cross_table().T, precision=lax.Precision.HIGHEST)
    return (results[0], results[1], results[2], results[3], shear_kernel)
```

```python
import functools

import jax
import jax.numpy as jnp
import numpy as np
from jax import lax
from jax.experimental import pallas as pl
from jax.experimental.pallas import tpu as pltpu
from jax.sharding import PartitionSpec as P

NGLL = 5
PXU = 16
PY = 33
PZ = 33
PYZ = 1089
NPTS = 17424
LANES = 1152

time_step = 0.02
cross_sigma = 1.5
cross_reach = 4

MESH = pl.DeviceIdType.MESH


def gll_tables():
    nodes = np.array([-1.0, -np.sqrt(3.0 / 7.0), 0.0, np.sqrt(3.0 / 7.0), 1.0])
    quad = np.array([0.1, 49.0 / 90.0, 32.0 / 45.0, 49.0 / 90.0, 0.1])
    bary = np.array(
        [1.0 / np.prod([nodes[a] - nodes[b] for b in range(5) if b != a]) for a in range(5)]
    )
    deriv = np.zeros((5, 5))
    for a in range(5):
        for b in range(5):
            if b != a:
                deriv[a, b] = bary[b] / bary[a] / (nodes[a] - nodes[b])
        deriv[a, a] = -np.sum(deriv[a])
    cube = (quad[:, None, None] * quad[None, :, None] * quad[None, None, :]).reshape(125)
    return deriv.astype(np.float32), cube.astype(np.float32)


DERIV, CUBE = gll_tables()
D = [[float(DERIV[a, b]) for b in range(5)] for a in range(5)]


def lane_tables():
    lane = np.arange(LANES)
    live = lane < PYZ
    y, z = lane // PZ, lane % PZ
    rows = []
    for pos, extent in ((y, PY), (z, PZ)):
        for d in range(-3, 5):
            node = pos % 4
            inside = live & (pos < extent - 1) & (node + d >= 0) & (node + d <= 4)
            value = DERIV[node, np.clip(node + d, 0, 4)]
            rows.append(np.where(inside, value, 0.0))
    for pos, extent in ((y, PY), (z, PZ)):
        weight = lambda d: np.exp(-d * d / (2.0 * cross_sigma * cross_sigma))
        norm = np.zeros(LANES)
        for d in range(-cross_reach, cross_reach + 1):
            norm += np.where((pos + d >= 0) & (pos + d < extent), weight(d), 0.0)
        for d in range(-cross_reach, cross_reach + 1):
            inside = live & (pos + d >= 0) & (pos + d < extent)
            rows.append(np.where(inside, weight(d) / norm, 0.0))
    rows = np.stack(rows).astype(np.float32)
    return np.pad(rows, ((0, 56 - rows.shape[0]), (0, 0)))


def band_table(events):
    sigma = PXU / 4.0
    w = lambda d: np.exp(-d * d / (2.0 * sigma * sigma))
    norm = np.sum(w(np.arange(-PXU, PXU + 1).astype(np.float64)))
    chunk = PXU // events
    table = np.zeros((events, 3, chunk, PXU))
    for e in range(events):
        for o in range(3):
            for r in range(chunk):
                gap = 16 * (o - 1) + chunk * e + r - np.arange(PXU)
                table[e, o, r] = np.where(np.abs(gap) <= PXU, w(gap.astype(np.float64)) / norm, 0.0)
    table = table.reshape(events * 3 * chunk, 4, 4).transpose(0, 2, 1)
    table = np.stack([table, np.zeros_like(table)], axis=2)
    return table.reshape(events * 3 * chunk, 2 * PXU).astype(np.float32)


def shifted(x, step):
    shift = (-step) % LANES
    return x if shift == 0 else pltpu.roll(x, shift, 1)


def stencil(u, coef_ref, base, stride):
    main = end = None
    for d in range(-4, 5):
        moved = shifted(u, stride * d)
        if d >= -3:
            row = base + d + 3
            term = coef_ref[row : row + 1, :] * moved
            main = term if main is None else main + term
        if d <= 0:
            term = D[4][4 + d] * moved
            end = term if end is None else end + term
    return main, end


def spread(fm, fe, coef_ref, base, stride):
    total = None
    for d in range(-4, 5):
        term = None
        if d >= -3:
            row = base + d + 3
            term = coef_ref[row : row + 1, :] * fm
        if d <= 0:
            part = D[4][4 + d] * fe
            term = part if term is None else term + part
        term = shifted(term, -stride * d)
        total = term if total is None else total + term
    return total


def step_kernel(
    events,
    slices,
    u_ref,
    v_ref,
    mass_ref,
    lhs_ref,
    base_ref,
    coef_ref,
    band_ref,
    un_ref,
    vn_ref,
    sk_ref,
    placed,
    ax,
    aym,
    aye,
    azm,
    aze,
    ghost,
    tail_u,
    tail_a,
    stage_g,
    stage_u,
    stage_a,
    force,
    kern,
    part,
    recv,
    rows,
    halo_send,
    halo_recv,
    part_send,
    part_recv,
    rows_send,
    rows_recv,
):
    chunk = PXU // events
    others = 3 * events - 1
    e = lax.axis_index("event")
    s = lax.axis_index("cuts")
    ahead, behind = lax.rem(s + 1, slices), lax.rem(s + slices - 1, slices)

    def partner(m):
        step = lax.rem(m + 1, 3)
        return {
            "event": lax.rem(e + (m + 1) // 3, events),
            "cuts": lax.rem(s + step + jnp.where(step == 2, slices - 3, 0), slices),
        }

    barrier = pltpu.get_barrier_semaphore()

    def greet(m, carry):
        pl.semaphore_signal(barrier, inc=1, device_id=partner(m), device_id_type=MESH)
        return carry

    lax.fori_loop(0, others, greet, 0)

    for f in range(2):
        stage_g[f : f + 1, :] = u_ref[4 * f : 4 * f + 1, :]
        for i in range(4):
            at = 8 * i + 4 * f + 3
            stage_u[2 * i + f : 2 * i + f + 1, :] = u_ref[at : at + 1, :]

    lhs = lhs_ref[...]
    hi = lhs.astype(jnp.bfloat16)
    rest = lhs - hi.astype(jnp.float32)
    mid = rest.astype(jnp.bfloat16)
    low = (rest - mid.astype(jnp.float32)).astype(jnp.bfloat16)
    lane = lax.broadcasted_iota(jnp.int32, (256, LANES), 1)
    pick = jnp.where(base_ref[...] == lane, 1.0, 0.0).astype(jnp.bfloat16)
    placed[...] = (
        jnp.dot(hi, pick, preferred_element_type=jnp.float32)
        + jnp.dot(mid, pick, preferred_element_type=jnp.float32)
        + jnp.dot(low, pick, preferred_element_type=jnp.float32)
    )

    pl.semaphore_wait(barrier, others)
    to_behind = pltpu.make_async_remote_copy(
        stage_g, ghost, halo_send.at[0], halo_recv.at[0], {"cuts": behind}, MESH
    )
    to_behind.start()
    to_ahead = pltpu.make_async_remote_copy(
        stage_u, tail_u, halo_send.at[1], halo_recv.at[1], {"cuts": ahead}, MESH
    )
    to_ahead.start()

    twice = lambda x: jnp.concatenate([x, x], axis=0)
    row = lax.broadcasted_iota(jnp.int32, (8, LANES), 0)
    kinds = (aym, aye, azm, aze)
    for c in (2, 0, 1):
        sums = [None] * 4
        for j in range(5):
            for k in range(5):
                first = 24 * (5 * j + k) + 8 * c
                moved = shifted(placed[first : first + 8, :], -(PZ * j + k))
                q = 2 * (j == 4) + (k == 4)
                sums[q] = moved if sums[q] is None else sums[q] + moved
        mm, me, em, ee = sums
        whole = (mm + me) + (em + ee)
        pairs = (mm + me, em + ee, mm + em, me + ee)
        if c == 2:
            ax[32:40, :] = twice(whole[0:4, :])
            for q in range(4):
                stage_a[4 + q : 5 + q, :] = sums[q][3:4, :]
                shifted_layer = pltpu.roll(twice(pairs[q][0:4, :]), 1, 0)
                kinds[q][0:8, :] = jnp.where(row % 4 == 0, 0.0, shifted_layer)
        else:
            for half in range(2):
                i = 2 * c + half
                some = slice(4 * half, 4 * half + 4)
                ax[8 * i : 8 * i + 8, :] = twice(whole[some, :])
                stage_a[i : i + 1, :] = whole[4 * half + 3 : 4 * half + 4, :]
                for q in range(4):
                    value = twice(pairs[q][some, :])
                    if i == 0:
                        value = value + kinds[q][0:8, :]
                    kinds[q][8 * i : 8 * i + 8, :] = value

    flux_ahead = pltpu.make_async_remote_copy(
        stage_a, tail_a, halo_send.at[2], halo_recv.at[2], {"cuts": ahead}, MESH
    )
    flux_ahead.start()

    for i in (1, 2, 3, 0):
        at = 8 * i
        if i == 0:
            flux_ahead.wait()
            mm, me, em, ee = (tail_a[4 + q : 5 + q, :] for q in range(4))
            for ref, value in zip(kinds, (mm + me, em + ee, mm + em, me + ee)):
                ref[0:1, :] += value
                ref[4:5, :] += value
        u = u_ref[at : at + 8, :]
        ksum = tsum = None
        for base, stride, m_ref, e_ref in ((0, PZ, aym, aye), (8, 1, azm, aze)):
            gm, ge = stencil(u, coef_ref, base, stride)
            fm, fe = m_ref[at : at + 8, :] * gm, e_ref[at : at + 8, :] * ge
            term = fm * pltpu.roll(gm, 4, 0) + fe * pltpu.roll(ge, 4, 0)
            ksum = term if ksum is None else ksum + term
            term = spread(fm, fe, coef_ref, base, stride)
            tsum = term if tsum is None else tsum + term
        kern[at : at + 8, :] = ksum
        force[at : at + 8, :] = tsum

    to_behind.wait()
    to_ahead.wait()
    slab = [u_ref[8 * i : 8 * i + 8, :] for i in range(4)]
    last = pltpu.roll(slab[0], 7, 0)
    last = jnp.where(row == 3, ghost[0:1, :], jnp.where(row == 7, ghost[1:2, :], last))
    slab.append(last)
    grads = []
    for a in range(5):
        total = None
        for b in range(5):
            term = D[a][b] * slab[b]
            total = term if total is None else total + term
        grads.append(total)
    moved = [ax[8 * a : 8 * a + 8, :] * grads[a] for a in range(5)]
    prods = [moved[a] * pltpu.roll(grads[a], 4, 0) for a in range(5)]
    turned = []
    for a in range(5):
        total = None
        for b in range(5):
            term = D[b][a] * moved[b]
            total = term if total is None else total + term
        turned.append(total)
    edge = [tail_u[2 * i : 2 * i + 2, :] for i in range(4)] + [stage_g[...]]
    edge_flux = [tail_a[i : i + 1, :] for i in range(4)]
    edge_flux.append(
        (tail_a[4:5, :] + tail_a[5:6, :]) + (tail_a[6:7, :] + tail_a[7:8, :])
    )
    edge_force = edge_kern = None
    for a in range(5):
        total = None
        for b in range(5):
            term = D[a][b] * edge[b]
            total = term if total is None else total + term
        term = (D[a][4] * edge_flux[a]) * total
        edge_force = term if edge_force is None else edge_force + term
        if a == 4:
            edge_kern = edge_flux[4] * total[0:1, :] * total[1:2, :]

    back = pltpu.roll(turned[4], 1, 0)
    back = jnp.where(row == 0, edge_force[0:1, :], jnp.where(row == 4, edge_force[1:2, :], back))
    turned[0] = turned[0] + back
    back = pltpu.roll(prods[4], 1, 0)
    back = jnp.where(row == 0, edge_kern, back)
    prods[0] = prods[0] + back
    for i in range(4):
        kern[8 * i : 8 * i + 8, :] += prods[i]
        force[8 * i : 8 * i + 8, :] += turned[i]

    added = jnp.dot(
        -band_ref[...],
        kern[...],
        precision=lax.Precision.HIGHEST,
        preferred_element_type=jnp.float32,
    )
    for m in range(3 * events):
        part[m] = added[chunk * m : chunk * m + chunk, :]

    def spray(m, carry):
        step = lax.rem(m + 1, 3)
        to = partner(m)
        slot = 3 * to["event"] + lax.rem(step + 1, 3)
        pltpu.make_async_remote_copy(
            part.at[slot], recv.at[m], part_send, part_recv, to, MESH
        ).start()
        return carry

    lax.fori_loop(0, others, spray, 0)

    for i in range(4):
        at = slice(8 * i, 8 * i + 8)
        step = jnp.where(row < 4, time_step, -time_step)
        speed = v_ref[at, :] + (step * mass_ref[at, :]) * force[at, :]
        vn_ref[at, :] = speed
        un_ref[at, :] = u_ref[at, :] - step * speed

    pltpu.make_async_copy(recv, recv, part_recv).wait()
    total = part[3 * e + 1]
    for m in range(others):
        total = total + recv[m]
    across = None
    for d in range(-cross_reach, cross_reach + 1):
        term = coef_ref[20 + d : 21 + d, :] * shifted(total, PZ * d)
        across = term if across is None else across + term
    total, across = across, None
    for d in range(-cross_reach, cross_reach + 1):
        term = coef_ref[29 + d : 30 + d, :] * shifted(total, d)
        across = term if across is None else across + term
    rows[e] = across

    def share(m, carry):
        to = {"event": lax.rem(e + m + 1, events)}
        pltpu.make_async_remote_copy(
            rows.at[e], rows.at[e], rows_send, rows_recv, to, MESH
        ).start()
        return carry

    lax.fori_loop(0, events - 1, share, 0)
    pltpu.make_async_copy(recv, recv, part_send).wait()
    some = rows.at[pl.ds(0, events - 1)]
    pltpu.make_async_copy(some, some, rows_recv).wait()
    pltpu.make_async_copy(some, some, rows_send).wait()
    for m in range(events):
        sk_ref[chunk * m : chunk * m + chunk, :] = rows[m]


def on_device(events, slices):
    def run(fd, fv, ad, av, inverse_mass, shear, connectivity, face_points, count):
        chunk = PXU // events
        layers = lambda x: jnp.pad(x.reshape(4, 4, PYZ), ((0, 0), (0, 0), (0, LANES - PYZ)))
        pair = lambda x, y: jnp.stack([layers(x), layers(y)]).transpose(2, 0, 1, 3).reshape(32, LANES)
        u = pair(fd[0], ad[0])
        v = pair(fv[0], av[0])
        mass = pair(inverse_mass, inverse_mass)
        first = connectivity[0]
        layer = first // (4 * PYZ)
        base = (first - 4 * PYZ * layer).reshape(256, 1)
        active = (jnp.arange(256, dtype=jnp.int32) < count[0]).astype(jnp.float32)
        flux = jnp.asarray(CUBE)[:, None] * shear * active[None, :]
        own = (layer[None, :] == jnp.arange(4, dtype=jnp.int32)[:, None]).astype(jnp.float32)
        cube = flux.reshape(5, 25, 256).transpose(1, 0, 2)
        lhs = (cube[:, :, None, :] * own[None, None, :, :]).reshape(25, 20, 256)
        lhs = jnp.pad(lhs, ((0, 0), (0, 4), (0, 0))).reshape(600, 256)
        vmem = pl.BlockSpec(memory_space=pltpu.VMEM)
        shape = jax.ShapeDtypeStruct
        f32 = jnp.float32
        big = lambda *dims: pltpu.VMEM((*dims, LANES), f32)
        un, vn, sk = pl.pallas_call(
            functools.partial(step_kernel, events, slices),
            out_shape=(shape((32, LANES), f32), shape((32, LANES), f32), shape((16, LANES), f32)),
            in_specs=[vmem] * 7,
            out_specs=(vmem, vmem, vmem),
            scratch_shapes=[
                big(600),
                big(40),
                big(32),
                big(32),
                big(32),
                big(32),
                big(2),
                big(8),
                big(8),
                big(2),
                big(8),
                big(8),
                big(32),
                big(32),
                big(3 * events, chunk),
                big(3 * events - 1, chunk),
                big(events, chunk),
                pltpu.SemaphoreType.DMA((3,)),
                pltpu.SemaphoreType.DMA((3,)),
                pltpu.SemaphoreType.DMA,
                pltpu.SemaphoreType.DMA,
                pltpu.SemaphoreType.DMA,
                pltpu.SemaphoreType.DMA,
            ],
            compiler_params=pltpu.CompilerParams(
                collective_id=0, has_side_effects=True, vmem_limit_bytes=40 << 20
            ),
        )(u, v, mass, lhs, base, jnp.asarray(lane_tables()), jnp.asarray(band_table(events)))
        def apart(x):
            x = x.reshape(4, 2, 4, LANES)[:, :, :, :PYZ].transpose(1, 2, 0, 3)
            return x[0].reshape(1, NPTS), x[1].reshape(1, NPTS)

        (fd, ad), (fv, av) = apart(un), apart(vn)
        return fd, fv, ad, av, sk[:, :PYZ]

    return run


def solution(mesh):
    both = P("event", "cuts")
    return jax.shard_map(
        on_device(mesh.shape["event"], mesh.shape["cuts"]),
        mesh=mesh,
        in_specs=(
            both,
            both,
            both,
            both,
            P("cuts"),
            P(None, "cuts"),
            P(None, "cuts"),
            P("cuts", None),
            P("cuts"),
        ),
        out_specs=(both, both, both, both, P("cuts", None)),
        check_vma=False,
    )
```

```python
import functools

import jax
import jax.numpy as jnp
import numpy as np
from jax import lax
from jax.experimental import pallas as pl
from jax.experimental.pallas import tpu as pltpu
from jax.sharding import PartitionSpec as P

NGLL = 5
PXU = 16
PY = 33
PZ = 33
PYZ = 1089
NPTS = 17424
LANES = 1152

time_step = 0.02
cross_sigma = 1.5
cross_reach = 4

MESH = pl.DeviceIdType.MESH


def gll_tables():
    nodes = np.array([-1.0, -np.sqrt(3.0 / 7.0), 0.0, np.sqrt(3.0 / 7.0), 1.0])
    quad = np.array([0.1, 49.0 / 90.0, 32.0 / 45.0, 49.0 / 90.0, 0.1])
    bary = np.array(
        [1.0 / np.prod([nodes[a] - nodes[b] for b in range(5) if b != a]) for a in range(5)]
    )
    deriv = np.zeros((5, 5))
    for a in range(5):
        for b in range(5):
            if b != a:
                deriv[a, b] = bary[b] / bary[a] / (nodes[a] - nodes[b])
        deriv[a, a] = -np.sum(deriv[a])
    cube = (quad[:, None, None] * quad[None, :, None] * quad[None, None, :]).reshape(125)
    return deriv.astype(np.float32), cube.astype(np.float32)


DERIV, CUBE = gll_tables()
D = [[float(DERIV[a, b]) for b in range(5)] for a in range(5)]


def lane_tables():
    lane = np.arange(LANES)
    live = lane < PYZ
    y, z = lane // PZ, lane % PZ
    rows = []
    for pos, extent in ((y, PY), (z, PZ)):
        for d in range(-3, 5):
            node = pos % 4
            inside = live & (pos < extent - 1) & (node + d >= 0) & (node + d <= 4)
            value = DERIV[node, np.clip(node + d, 0, 4)]
            rows.append(np.where(inside, value, 0.0))
    for pos, extent in ((y, PY), (z, PZ)):
        weight = lambda d: np.exp(-d * d / (2.0 * cross_sigma * cross_sigma))
        norm = np.zeros(LANES)
        for d in range(-cross_reach, cross_reach + 1):
            norm += np.where((pos + d >= 0) & (pos + d < extent), weight(d), 0.0)
        for d in range(-cross_reach, cross_reach + 1):
            inside = live & (pos + d >= 0) & (pos + d < extent)
            rows.append(np.where(inside, weight(d) / norm, 0.0))
    rows = np.stack(rows).astype(np.float32)
    return np.pad(rows, ((0, 56 - rows.shape[0]), (0, 0)))


def band_table():
    sigma = PXU / 4.0
    w = lambda d: np.exp(-d * d / (2.0 * sigma * sigma))
    norm = np.sum(w(np.arange(-PXU, PXU + 1).astype(np.float64)))
    gap = np.arange(-PXU, 2 * PXU)[None, :] - np.arange(PXU)[:, None]
    table = np.where(np.abs(gap) <= PXU, w(gap.astype(np.float64)) / norm, 0.0)
    table = table.reshape(PXU, 3, 4, 4).transpose(0, 1, 3, 2).reshape(PXU, 48)
    return np.pad(-table, ((0, 0), (0, 80))).astype(np.float32)


def shifted(x, step):
    shift = (-step) % LANES
    return x if shift == 0 else pltpu.roll(x, shift, 1)


def stencil(u, coef_ref, base, stride):
    main = end = None
    for d in range(-4, 5):
        moved = shifted(u, stride * d)
        if d >= -3:
            row = base + d + 3
            term = coef_ref[row : row + 1, :] * moved
            main = term if main is None else main + term
        if d <= 0:
            term = D[4][4 + d] * moved
            end = term if end is None else end + term
    return main, end


def spread(fm, fe, coef_ref, base, stride):
    total = None
    for d in range(-4, 5):
        term = None
        if d >= -3:
            row = base + d + 3
            term = coef_ref[row : row + 1, :] * fm
        if d <= 0:
            part = D[4][4 + d] * fe
            term = part if term is None else term + part
        term = shifted(term, -stride * d)
        total = term if total is None else total + term
    return total


FIRST = [PYZ * i // 128 for i in range(4)]
LEAD = [PYZ * i % 128 for i in range(4)]
GROUP = 34


def lane_starts(i, lane_row):
    return LEAD[i] + 4 * (lane_row % 4)


def run_of(flat_ref, start, size):
    if len(flat_ref.shape) == 1:
        return flat_ref[start : start + size]
    return flat_ref[0:1, start : start + size]


def flat_to_rows(flat_ref, both, first):
    for g in range(17):
        both[first + 8 * g : first + 8 * g + 8, :] = run_of(flat_ref, 1024 * g, 1024).reshape(8, 128)


def planes(both, tail_row, i, lane, row):
    tiles = []
    for t in range(10):
        at = FIRST[i] + t
        tile = both[pl.ds(at, 8, stride=GROUP), :]
        if i == 3 and t == 9:
            tile = jnp.where(row == 3, tail_row, tile)
        if LEAD[i]:
            tile = pltpu.roll(tile, 128 - LEAD[i], 1)
        tile = jnp.where(row % 2 == 1, pltpu.roll(tile, 124, 1), tile)
        tiles.append(jnp.where(row % 4 >= 2, pltpu.roll(tile, 120, 1), tile))
    keep = lane < 128 - lane_starts(i, row)
    return jnp.concatenate([jnp.where(keep, tiles[t], tiles[t + 1]) for t in range(9)], axis=1)


def planes_to_flat(slabs, out_refs, rows_refs, lane, row):
    before = None
    done = []
    for i in range(4):
        tiles = []
        for t in range(9):
            tile = slabs[i][:, 128 * t : 128 * t + 128]
            if LEAD[i]:
                tile = pltpu.roll(tile, LEAD[i], 1)
            tile = jnp.where(row % 2 == 1, pltpu.roll(tile, 4, 1), tile)
            tiles.append(jnp.where(row % 4 >= 2, pltpu.roll(tile, 8, 1), tile))
        start = lane < lane_starts(i, row)
        count = (FIRST + [GROUP])[i + 1] - FIRST[i]
        for t in range(count):
            low = tiles[t - 1] if t else before
            done.append(tiles[t] if low is None else jnp.where(start, low, tiles[t]))
        before = tiles[8] if count == 9 else jnp.where(start, tiles[7], tiles[8])
    done[0] = jnp.where(lane < lane_starts(0, row), pltpu.roll(before, 1, 0), done[0])
    for f in range(2):
        rows = rows_refs[f]
        for g in range(GROUP):
            rows[pl.ds(g, 4, stride=GROUP), :] = done[g][4 * f : 4 * f + 4, :]
        for g in range(17):
            out_refs[f][0:1, 1024 * g : 1024 * g + 1024] = rows[8 * g : 8 * g + 8, :].reshape(1, 1024)
        out_refs[f][0:1, 17408:17424] = before[4 * f + 3 : 4 * f + 4, 0:16]


def step_kernel(
    events,
    slices,
    fd_hbm,
    fv_hbm,
    ad_hbm,
    av_hbm,
    mass_hbm,
    shear_hbm,
    conn_hbm,
    count_ref,
    coef_hbm,
    band_hbm,
    fdn_ref,
    fvn_ref,
    adn_ref,
    avn_ref,
    sk_ref,
    flats,
    mass_flat,
    both,
    tails,
    rows_a,
    rows_b,
    shear_ref,
    conn_ref,
    coef_ref,
    band_ref,
    u_ref,
    lhs,
    placed,
    ax,
    aym,
    aye,
    azm,
    aze,
    ghost,
    tail_u,
    tail_a,
    stage_g,
    stage_u,
    stage_a,
    force,
    kern,
    part,
    recv,
    total_ref,
    halo,
    cols,
    load_sem,
    halo_send,
    halo_recv,
    part_send,
    part_recv,
    edge_send,
    edge_recv,
    cols_send,
    cols_recv,
):
    f32 = jnp.float32
    e = lax.axis_index("event")
    s = lax.axis_index("cuts")
    ahead, behind = lax.rem(s + 1, slices), lax.rem(s + slices - 1, slices)

    barrier = pltpu.get_barrier_semaphore()
    for to in (ahead, behind):
        pl.semaphore_signal(barrier, inc=1, device_id={"cuts": to}, device_id_type=MESH)

    def event_at(m):
        return {"event": lax.rem(e + m, events)}

    for m in range(1, events):
        pl.semaphore_signal(barrier, inc=1, device_id=event_at(m), device_id_type=MESH)

    loads = [
        pltpu.make_async_copy(src, dst, load_sem.at[n])
        for n, (src, dst) in enumerate(
            (
                (fd_hbm, flats.at[0]),
                (ad_hbm, flats.at[1]),
                (conn_hbm.at[pl.ds(0, 8), :], conn_ref),
                (shear_hbm, shear_ref),
                (coef_hbm, coef_ref),
                (fv_hbm, flats.at[2]),
                (av_hbm, flats.at[3]),
                (mass_hbm, mass_flat),
                (band_hbm, band_ref),
            )
        )
    ]
    for load in loads:
        load.start()

    row = lax.broadcasted_iota(jnp.int32, (8, LANES), 0)
    row1 = lax.broadcasted_iota(jnp.int32, (8, 128), 0)
    lane1 = lax.broadcasted_iota(jnp.int32, (8, 128), 1)

    def slabs_of(first, second):
        flat_to_rows(first, both, 0)
        flat_to_rows(second, both, 136)
        tails[...] = jnp.zeros((8, 128), f32)
        tails[0:1, 0:16] = run_of(first, 17408, 16).reshape(1, 16)
        both[272:280, :] = jnp.zeros((8, 128), f32)
        both[272:273, 0:16] = run_of(second, 17408, 16).reshape(1, 16)
        return [planes(both, tails[0:1, :], i, lane1, row1) for i in range(4)]

    loads[0].wait()
    loads[1].wait()
    for i, value in enumerate(slabs_of(flats.at[0], flats.at[1])):
        u_ref[8 * i : 8 * i + 8, :] = value
    for f in range(2):
        stage_g[f : f + 1, :] = u_ref[4 * f : 4 * f + 1, :]
        for i in range(4):
            at = 8 * i + 4 * f + 3
            stage_u[2 * i + f : 2 * i + f + 1, :] = u_ref[at : at + 1, :]

    pl.semaphore_wait(barrier, events + 1)
    to_behind = pltpu.make_async_remote_copy(
        stage_g, ghost, halo_send.at[0], halo_recv.at[0], {"cuts": behind}, MESH
    )
    to_behind.start()
    to_ahead = pltpu.make_async_remote_copy(
        stage_u, tail_u, halo_send.at[1], halo_recv.at[1], {"cuts": ahead}, MESH
    )
    to_ahead.start()

    for n in (2, 3):
        loads[n].wait()
    first = conn_ref[0:1, :]
    layer = sum(jnp.where(first >= 4 * PYZ * n, 1, 0) for n in (1, 2, 3))
    base = jnp.broadcast_to(first - 4 * PYZ * layer, (128, 256)).T
    wide_row = lax.broadcasted_iota(jnp.int32, (8, 256), 0)
    slot = lax.broadcasted_iota(jnp.int32, (8, 256), 1)
    own = jnp.where((wide_row % 4 == layer) & (slot < count_ref[0]), 1.0, 0.0)

    def flux_rows(c, jk):
        if jk == 25:
            return jnp.zeros((8, 256), f32)
        near = 50 * c + jk
        value = float(CUBE[near]) * shear_ref[near : near + 1, :]
        if c < 2:
            far = near + 25
            value = jnp.where(wide_row < 4, value, float(CUBE[far]) * shear_ref[far : far + 1, :])
        else:
            value = jnp.where(wide_row < 4, value, 0.0)
        return value * own

    for c in range(3):
        for pair in range(13):
            value = jnp.concatenate([flux_rows(c, 2 * pair), flux_rows(c, 2 * pair + 1)], axis=0)
            at = 208 * c + 16 * pair
            hi = value.astype(jnp.bfloat16)
            rest = value - hi.astype(f32)
            mid = rest.astype(jnp.bfloat16)
            lhs[0, at : at + 16, :] = hi
            lhs[1, at : at + 16, :] = mid
            lhs[2, at : at + 16, :] = (rest - mid.astype(f32)).astype(jnp.bfloat16)
    lane_wide = lax.broadcasted_iota(jnp.int32, (256, 128), 1)
    pick = jnp.concatenate(
        [jnp.where(base == lane_wide + 128 * t, 1.0, 0.0).astype(jnp.bfloat16) for t in range(9)], axis=1
    )
    placed[...] = (
        jnp.dot(lhs[0], pick, preferred_element_type=f32)
        + jnp.dot(lhs[1], pick, preferred_element_type=f32)
        + jnp.dot(lhs[2], pick, preferred_element_type=f32)
    )

    twice = lambda x: jnp.concatenate([x, x], axis=0)
    kinds = (aym, aye, azm, aze)
    for c in (2, 0, 1):
        sums = [None] * 4
        for j in range(5):
            for k in range(5):
                at = 208 * c + 8 * (5 * j + k)
                moved = shifted(placed[at : at + 8, :], -(PZ * j + k))
                q = 2 * (j == 4) + (k == 4)
                sums[q] = moved if sums[q] is None else sums[q] + moved
        mm, me, em, ee = sums
        whole = (mm + me) + (em + ee)
        pairs = (mm + me, em + ee, mm + em, me + ee)
        if c == 2:
            ax[32:40, :] = twice(whole[0:4, :])
            for q in range(4):
                stage_a[4 + q : 5 + q, :] = sums[q][3:4, :]
                shifted_layer = pltpu.roll(twice(pairs[q][0:4, :]), 1, 0)
                kinds[q][0:8, :] = jnp.where(row % 4 == 0, 0.0, shifted_layer)
        else:
            for half in range(2):
                i = 2 * c + half
                some = slice(4 * half, 4 * half + 4)
                ax[8 * i : 8 * i + 8, :] = twice(whole[some, :])
                stage_a[i : i + 1, :] = whole[4 * half + 3 : 4 * half + 4, :]
                for q in range(4):
                    value = twice(pairs[q][some, :])
                    if i == 0:
                        value = value + kinds[q][0:8, :]
                    kinds[q][8 * i : 8 * i + 8, :] = value

    flux_ahead = pltpu.make_async_remote_copy(
        stage_a, tail_a, halo_send.at[2], halo_recv.at[2], {"cuts": ahead}, MESH
    )
    flux_ahead.start()

    loads[4].wait()
    for i in (1, 2, 3, 0):
        at = 8 * i
        if i == 0:
            flux_ahead.wait()
            mm, me, em, ee = (tail_a[4 + q : 5 + q, :] for q in range(4))
            for ref, value in zip(kinds, (mm + me, em + ee, mm + em, me + ee)):
                ref[0:1, :] += value
                ref[4:5, :] += value
        u = u_ref[at : at + 8, :]
        ksum = tsum = None
        for base, stride, m_ref, e_ref in ((0, PZ, aym, aye), (8, 1, azm, aze)):
            gm, ge = stencil(u, coef_ref, base, stride)
            fm, fe = m_ref[at : at + 8, :] * gm, e_ref[at : at + 8, :] * ge
            term = fm * pltpu.roll(gm, 4, 0) + fe * pltpu.roll(ge, 4, 0)
            ksum = term if ksum is None else ksum + term
            term = spread(fm, fe, coef_ref, base, stride)
            tsum = term if tsum is None else tsum + term
        kern[at : at + 8, :] = ksum
        force[at : at + 8, :] = tsum

    to_behind.wait()
    to_ahead.wait()
    slab = [u_ref[8 * i : 8 * i + 8, :] for i in range(4)]
    last = pltpu.roll(slab[0], 7, 0)
    last = jnp.where(row == 3, ghost[0:1, :], jnp.where(row == 7, ghost[1:2, :], last))
    slab.append(last)
    grads = []
    for a in range(5):
        total = None
        for b in range(5):
            term = D[a][b] * slab[b]
            total = term if total is None else total + term
        grads.append(total)
    moved = [ax[8 * a : 8 * a + 8, :] * grads[a] for a in range(5)]
    prods = [moved[a] * pltpu.roll(grads[a], 4, 0) for a in range(5)]
    turned = []
    for a in range(5):
        total = None
        for b in range(5):
            term = D[b][a] * moved[b]
            total = term if total is None else total + term
        turned.append(total)
    edge = [tail_u[2 * i : 2 * i + 2, :] for i in range(4)] + [stage_g[...]]
    edge_flux = [tail_a[i : i + 1, :] for i in range(4)]
    edge_flux.append(
        (tail_a[4:5, :] + tail_a[5:6, :]) + (tail_a[6:7, :] + tail_a[7:8, :])
    )
    edge_force = edge_kern = None
    for a in range(5):
        total = None
        for b in range(5):
            term = D[a][b] * edge[b]
            total = term if total is None else total + term
        term = (D[a][4] * edge_flux[a]) * total
        edge_force = term if edge_force is None else edge_force + term
        if a == 4:
            edge_kern = edge_flux[4] * total[0:1, :] * total[1:2, :]

    back = pltpu.roll(turned[4], 1, 0)
    back = jnp.where(row == 0, edge_force[0:1, :], jnp.where(row == 4, edge_force[1:2, :], back))
    turned[0] = turned[0] + back
    back = pltpu.roll(prods[4], 1, 0)
    back = jnp.where(row == 0, edge_kern, back)
    prods[0] = prods[0] + back
    for i in range(4):
        kern[8 * i : 8 * i + 8, :] += prods[i]
        force[8 * i : 8 * i + 8, :] += turned[i]

    for half in range(2):
        both_nodes = jnp.where(
            row < 4, kern[16 * half : 16 * half + 8, :], kern[16 * half + 8 : 16 * half + 16, :]
        )
        for m in range(events):
            part[m, 8 * half : 8 * half + 8, :] = both_nodes[:, 128 * m : 128 * m + 128]
            part[m, 16 + 8 * half : 24 + 8 * half, :] = both_nodes[:, 128 * events : LANES]
    for m in range(1, events):
        to = event_at(m)
        pltpu.make_async_remote_copy(
            part.at[to["event"]], recv.at[m - 1], part_send, part_recv, to, MESH
        ).start()

    for n in (5, 6, 7, 8):
        loads[n].wait()
    mass = slabs_of(mass_flat, mass_flat)
    sign = jnp.where(row < 4, time_step, -time_step)
    speeds = [
        speed + (sign * mass[i]) * force[8 * i : 8 * i + 8, :] for i, speed in enumerate(slabs_of(flats.at[2], flats.at[3]))
    ]
    planes_to_flat(speeds, (fvn_ref, avn_ref), (rows_a, rows_b), lane1, row1)
    moved = [u_ref[8 * i : 8 * i + 8, :] - sign * speeds[i] for i in range(4)]
    planes_to_flat(moved, (fdn_ref, adn_ref), (rows_a, rows_b), lane1, row1)

    pltpu.make_async_copy(recv, recv, part_recv).wait()
    total = part[e]
    for m in range(events - 1):
        total = total + recv[m]
    total_ref[...] = total
    edges = [
        pltpu.make_async_remote_copy(
            total_ref, halo.at[n], edge_send.at[n], edge_recv.at[n], {"cuts": to}, MESH
        )
        for n, to in enumerate((ahead, behind))
    ]
    for edge in edges:
        edge.start()
    for edge in edges:
        edge.wait()
    tall = lambda at: jnp.concatenate(
        [halo[0, at : at + 16, :], total_ref[at : at + 16, :], halo[1, at : at + 16, :]], axis=0
    )
    along = jnp.dot(
        band_ref[:, 0:48],
        jnp.concatenate([tall(0), tall(16)], axis=1),
        precision=lax.Precision.HIGHEST,
        preferred_element_type=f32,
    )
    cols[e] = along[:, 0:128]
    for m in range(1, events):
        pltpu.make_async_remote_copy(cols.at[e], cols.at[e], cols_send, cols_recv, event_at(m), MESH).start()
    pltpu.make_async_copy(recv, recv, part_send).wait()
    some = cols.at[pl.ds(0, events - 1)]
    pltpu.make_async_copy(some, some, cols_recv).wait()
    total = jnp.concatenate([cols[m] for m in range(events)] + [along[:, 128:256]], axis=1)
    across = None
    for d in range(-cross_reach, cross_reach + 1):
        term = coef_ref[20 + d : 21 + d, :] * shifted(total, PZ * d)
        across = term if across is None else across + term
    total, across = across, None
    for d in range(-cross_reach, cross_reach + 1):
        term = coef_ref[29 + d : 30 + d, :] * shifted(total, d)
        across = term if across is None else across + term
    sk_ref[...] = across[:, 0:PYZ]
    pltpu.make_async_copy(some, some, cols_send).wait()


def store_kernel(a, b, c, d, k, a_hbm, b_hbm, c_hbm, d_hbm, k_hbm, sem):
    pairs = ((k, k_hbm), (a, a_hbm), (b, b_hbm), (c, c_hbm), (d, d_hbm))
    copies = [pltpu.make_async_copy(src, dst, sem.at[n]) for n, (src, dst) in enumerate(pairs)]
    for copy in copies:
        copy.start()
    for copy in copies:
        copy.wait()


def on_device(events, slices):
    def run(fd, fv, ad, av, inverse_mass, shear, connectivity, face_points, count):
        vmem = pl.BlockSpec(memory_space=pltpu.VMEM)
        there = pl.BlockSpec(memory_space=pltpu.HBM)
        stay = lambda x: pltpu.with_memory_space_constraint(x, pltpu.HBM)
        f32 = jnp.float32
        flat = jax.ShapeDtypeStruct((1, NPTS), f32)
        table = jax.ShapeDtypeStruct((PXU, PYZ), f32)
        big = lambda *dims: pltpu.VMEM((*dims, LANES), f32)
        small = lambda *dims: pltpu.VMEM((*dims, 128), f32)
        dma = pltpu.SemaphoreType.DMA
        outs = pl.pallas_call(
            functools.partial(step_kernel, events, slices),
            out_shape=(flat, flat, flat, flat, table),
            in_specs=[there] * 7 + [pl.BlockSpec(memory_space=pltpu.SMEM)] + [there] * 2,
            out_specs=(vmem,) * 5,
            scratch_shapes=[
                pltpu.VMEM((4, 1, NPTS), f32),
                pltpu.VMEM((NPTS,), f32),
                small(280),
                small(8),
                small(136),
                small(136),
                pltpu.VMEM((125, 256), f32),
                pltpu.VMEM((8, 256), jnp.int32),
                big(56),
                small(16),
                big(32),
                pltpu.VMEM((3, 624, 256), jnp.bfloat16),
                big(624),
                big(40),
                big(32),
                big(32),
                big(32),
                big(32),
                big(2),
                big(8),
                big(8),
                big(2),
                big(8),
                big(8),
                big(32),
                big(32),
                small(events, 32),
                small(events - 1, 32),
                small(32),
                small(2, 32),
                small(events, 16),
                dma((9,)),
                dma((3,)),
                dma((3,)),
                dma,
                dma,
                dma((2,)),
                dma((2,)),
                dma,
                dma,
            ],
            compiler_params=pltpu.CompilerParams(
                collective_id=0, has_side_effects=True, vmem_limit_bytes=40 << 20
            ),
        )(
            *map(stay, (fd, fv, ad, av, inverse_mass, shear, connectivity)),
            count,
            stay(jnp.asarray(lane_tables())),
            stay(jnp.asarray(band_table())),
        )
        fdn, fvn, adn, avn, sk = pl.pallas_call(
            store_kernel,
            out_shape=(flat, flat, flat, flat, table),
            in_specs=[vmem] * 5,
            out_specs=(there,) * 5,
            scratch_shapes=[dma((5,))],
            compiler_params=pltpu.CompilerParams(vmem_limit_bytes=4 << 20),
        )(*outs)
        return fdn, fvn, adn, avn, sk

    return run


def solution(mesh):
    both = P("event", "cuts")
    return jax.shard_map(
        on_device(mesh.shape["event"], mesh.shape["cuts"]),
        mesh=mesh,
        in_specs=(
            both,
            both,
            both,
            both,
            P("cuts"),
            P(None, "cuts"),
            P(None, "cuts"),
            P("cuts", None),
            P("cuts"),
        ),
        out_specs=(both, both, both, both, P("cuts", None)),
        check_vma=False,
    )
```

```python
import functools

import jax
import jax.numpy as jnp
import numpy as np
from jax import lax
from jax.experimental import pallas as pl
from jax.experimental.pallas import tpu as pltpu
from jax.sharding import PartitionSpec as P

NGLL = 5
PXU = 16
PY = 33
PZ = 33
PYZ = 1089
NPTS = 17424
LANES = 1152

time_step = 0.02
cross_sigma = 1.5
cross_reach = 4

MESH = pl.DeviceIdType.MESH


def gll_tables():
    nodes = np.array([-1.0, -np.sqrt(3.0 / 7.0), 0.0, np.sqrt(3.0 / 7.0), 1.0])
    quad = np.array([0.1, 49.0 / 90.0, 32.0 / 45.0, 49.0 / 90.0, 0.1])
    bary = np.array(
        [1.0 / np.prod([nodes[a] - nodes[b] for b in range(5) if b != a]) for a in range(5)]
    )
    deriv = np.zeros((5, 5))
    for a in range(5):
        for b in range(5):
            if b != a:
                deriv[a, b] = bary[b] / bary[a] / (nodes[a] - nodes[b])
        deriv[a, a] = -np.sum(deriv[a])
    cube = (quad[:, None, None] * quad[None, :, None] * quad[None, None, :]).reshape(125)
    return deriv.astype(np.float32), cube.astype(np.float32)


DERIV, CUBE = gll_tables()
D = [[float(DERIV[a, b]) for b in range(5)] for a in range(5)]


def lane_tables():
    lane = np.arange(LANES)
    live = lane < PYZ
    y, z = lane // PZ, lane % PZ
    rows = []
    for pos, extent in ((y, PY), (z, PZ)):
        for d in range(-3, 5):
            node = pos % 4
            inside = live & (pos < extent - 1) & (node + d >= 0) & (node + d <= 4)
            value = DERIV[node, np.clip(node + d, 0, 4)]
            rows.append(np.where(inside, value, 0.0))
    for pos, extent in ((y, PY), (z, PZ)):
        weight = lambda d: np.exp(-d * d / (2.0 * cross_sigma * cross_sigma))
        norm = np.zeros(LANES)
        for d in range(-cross_reach, cross_reach + 1):
            norm += np.where((pos + d >= 0) & (pos + d < extent), weight(d), 0.0)
        for d in range(-cross_reach, cross_reach + 1):
            inside = live & (pos + d >= 0) & (pos + d < extent)
            rows.append(np.where(inside, weight(d) / norm, 0.0))
    rows = np.stack(rows).astype(np.float32)
    return np.pad(rows, ((0, 56 - rows.shape[0]), (0, 0)))


def band_table():
    sigma = PXU / 4.0
    w = lambda d: np.exp(-d * d / (2.0 * sigma * sigma))
    norm = np.sum(w(np.arange(-PXU, PXU + 1).astype(np.float64)))

    def table(places):
        gap = places[None, :] - np.arange(PXU)[:, None]
        return np.where(np.abs(gap) <= PXU, w(gap.astype(np.float64)) / norm, 0.0)

    rows = table(np.arange(-PXU, 2 * PXU)).reshape(PXU, 3, 4, 4).transpose(0, 1, 3, 2).reshape(PXU, 48)
    places = PXU * np.arange(-2, 3)[:, None] + np.array([-4, -3, -2, -1, 16])[None, :]
    extra = np.pad(table(places.reshape(25)).reshape(PXU, 5, 5), ((0, 0), (0, 0), (0, 3)))
    both = np.concatenate([rows, extra.reshape(PXU, 40)], axis=1)
    return np.pad(-both, ((0, 0), (0, 40))).astype(np.float32)


def shifted(x, step):
    shift = (-step) % LANES
    return x if shift == 0 else pltpu.roll(x, shift, 1)


def stencil(u, coef_ref, base, stride):
    main = end = None
    for d in range(-4, 5):
        moved = shifted(u, stride * d)
        if d >= -3:
            row = base + d + 3
            term = coef_ref[row : row + 1, :] * moved
            main = term if main is None else main + term
        if d <= 0:
            term = D[4][4 + d] * moved
            end = term if end is None else end + term
    return main, end


def spread(fm, fe, coef_ref, base, stride):
    total = None
    for d in range(-4, 5):
        term = None
        if d >= -3:
            row = base + d + 3
            term = coef_ref[row : row + 1, :] * fm
        if d <= 0:
            part = D[4][4 + d] * fe
            term = part if term is None else term + part
        term = shifted(term, -stride * d)
        total = term if total is None else total + term
    return total


FIRST = [PYZ * i // 128 for i in range(4)]
LEAD = [PYZ * i % 128 for i in range(4)]
GROUP = 34


def lane_starts(i, lane_row):
    return LEAD[i] + 4 * (lane_row % 4)


def run_of(flat_ref, start, size):
    if len(flat_ref.shape) == 1:
        return flat_ref[start : start + size]
    return flat_ref[0:1, start : start + size]


def flat_to_rows(flat_ref, both, first):
    for g in range(17):
        both[first + 8 * g : first + 8 * g + 8, :] = run_of(flat_ref, 1024 * g, 1024).reshape(8, 128)


def planes(both, tail_row, i, lane, row):
    tiles = []
    for t in range(10):
        at = FIRST[i] + t
        tile = both[pl.ds(at, 8, stride=GROUP), :]
        if i == 3 and t == 9:
            tile = jnp.where(row == 3, tail_row, tile)
        if LEAD[i]:
            tile = pltpu.roll(tile, 128 - LEAD[i], 1)
        tile = jnp.where(row % 2 == 1, pltpu.roll(tile, 124, 1), tile)
        tiles.append(jnp.where(row % 4 >= 2, pltpu.roll(tile, 120, 1), tile))
    keep = lane < 128 - lane_starts(i, row)
    return jnp.concatenate([jnp.where(keep, tiles[t], tiles[t + 1]) for t in range(9)], axis=1)


def planes_to_flat(slabs, rows_refs, lane, row):
    before = None
    done = []
    for i in range(4):
        tiles = []
        for t in range(9):
            tile = slabs[i][:, 128 * t : 128 * t + 128]
            if LEAD[i]:
                tile = pltpu.roll(tile, LEAD[i], 1)
            tile = jnp.where(row % 2 == 1, pltpu.roll(tile, 4, 1), tile)
            tiles.append(jnp.where(row % 4 >= 2, pltpu.roll(tile, 8, 1), tile))
        start = lane < lane_starts(i, row)
        count = (FIRST + [GROUP])[i + 1] - FIRST[i]
        for t in range(count):
            low = tiles[t - 1] if t else before
            done.append(tiles[t] if low is None else jnp.where(start, low, tiles[t]))
        before = tiles[8] if count == 9 else jnp.where(start, tiles[7], tiles[8])
    done[0] = jnp.where(lane < lane_starts(0, row), pltpu.roll(before, 1, 0), done[0])
    for f in range(2):
        rows = rows_refs[f]
        for g in range(GROUP):
            rows[pl.ds(g, 4, stride=GROUP), :] = done[g][4 * f : 4 * f + 4, :]
    return [before[4 * f + 3 : 4 * f + 4, 0:16] for f in range(2)]


def step_kernel(
    events,
    slices,
    fd_hbm,
    fv_hbm,
    ad_hbm,
    av_hbm,
    mass_hbm,
    shear_hbm,
    conn_hbm,
    count_ref,
    coef_hbm,
    band_hbm,
    fdn_ref,
    fvn_ref,
    adn_ref,
    avn_ref,
    sk_ref,
    flats,
    mass_flat,
    both,
    tails,
    rows_a,
    rows_b,
    shear_ref,
    conn_ref,
    coef_ref,
    band_ref,
    u_ref,
    lhs,
    placed,
    ax,
    aym,
    aye,
    azm,
    aze,
    carried,
    returned,
    ghost,
    tail_u,
    tail_a,
    stage_g,
    stage_f,
    stage_r,
    stage_u,
    stage_a,
    force,
    kern,
    part,
    recv,
    recv_short,
    total_ref,
    halo,
    halo_far,
    cols,
    lone,
    load_sem,
    halo_send,
    halo_recv,
    part_send,
    part_recv,
    short_send,
    short_recv,
    edge_send,
    edge_recv,
    cols_send,
    cols_recv,
    lone_send,
    lone_recv,
):
    f32 = jnp.float32
    e = lax.axis_index("event")
    s = lax.axis_index("cuts")
    first, final = s == 0, s == slices - 1
    cut_at = lambda m: {"cuts": lax.rem(s + m + slices, slices)}

    barrier = pltpu.get_barrier_semaphore()
    for m in (-1, 1, -2, 2):
        pl.semaphore_signal(barrier, inc=1, device_id=cut_at(m), device_id_type=MESH)

    def event_at(m):
        return {"event": lax.rem(e + m, events)}

    for m in range(1, events):
        pl.semaphore_signal(barrier, inc=1, device_id=event_at(m), device_id_type=MESH)

    loads = [
        pltpu.make_async_copy(src, dst, load_sem.at[n])
        for n, (src, dst) in enumerate(
            (
                (conn_hbm.at[pl.ds(0, 8), :], conn_ref),
                (shear_hbm, shear_ref),
                (fd_hbm, flats.at[0]),
                (ad_hbm, flats.at[1]),
                (coef_hbm, coef_ref),
                (fv_hbm, flats.at[2]),
                (av_hbm, flats.at[3]),
                (mass_hbm, mass_flat),
                (band_hbm, band_ref),
            )
        )
    ]
    for load in loads:
        load.start()

    row = lax.broadcasted_iota(jnp.int32, (8, LANES), 0)
    row1 = lax.broadcasted_iota(jnp.int32, (8, 128), 0)
    lane1 = lax.broadcasted_iota(jnp.int32, (8, 128), 1)

    def slabs_of(first, second):
        flat_to_rows(first, both, 0)
        flat_to_rows(second, both, 136)
        tails[...] = jnp.zeros((8, 128), f32)
        tails[0:1, 0:16] = run_of(first, 17408, 16).reshape(1, 16)
        both[272:280, :] = jnp.zeros((8, 128), f32)
        both[272:273, 0:16] = run_of(second, 17408, 16).reshape(1, 16)
        return [planes(both, tails[0:1, :], i, lane1, row1) for i in range(4)]

    for n in (0, 1):
        loads[n].wait()
    corner = conn_ref[0:1, :]
    layer = sum(jnp.where(corner >= 4 * PYZ * n, 1, 0) for n in (1, 2, 3))
    base = jnp.broadcast_to(corner - 4 * PYZ * layer, (128, 256)).T
    wide_row = lax.broadcasted_iota(jnp.int32, (8, 256), 0)
    slot = lax.broadcasted_iota(jnp.int32, (8, 256), 1)
    own = jnp.where((wide_row % 4 == layer) & (slot < count_ref[0]), 1.0, 0.0)

    def flux_rows(c, jk):
        if jk == 25:
            return jnp.zeros((8, 256), f32)
        near = 50 * c + jk
        value = float(CUBE[near]) * shear_ref[near : near + 1, :]
        if c < 2:
            far = near + 25
            value = jnp.where(wide_row < 4, value, float(CUBE[far]) * shear_ref[far : far + 1, :])
        else:
            value = jnp.where(wide_row < 4, value, 0.0)
        return value * own

    for c in range(3):
        for pair in range(13):
            value = jnp.concatenate([flux_rows(c, 2 * pair), flux_rows(c, 2 * pair + 1)], axis=0)
            at = 208 * c + 16 * pair
            hi = value.astype(jnp.bfloat16)
            lhs[0, at : at + 16, :] = hi
            lhs[1, at : at + 16, :] = (value - hi.astype(f32)).astype(jnp.bfloat16)
    lane_wide = lax.broadcasted_iota(jnp.int32, (256, 128), 1)
    pick = jnp.concatenate(
        [jnp.where(base == lane_wide + 128 * t, 1.0, 0.0).astype(jnp.bfloat16) for t in range(9)], axis=1
    )
    placed[...] = jnp.dot(lhs[0], pick, preferred_element_type=f32) + jnp.dot(
        lhs[1], pick, preferred_element_type=f32
    )

    loads[2].wait()
    loads[3].wait()
    for i, value in enumerate(slabs_of(flats.at[0], flats.at[1])):
        u_ref[8 * i : 8 * i + 8, :] = value
    for f in range(2):
        stage_g[f : f + 1, :] = u_ref[4 * f : 4 * f + 1, :]
        for i in range(4):
            at = 8 * i + 4 * f + 3
            stage_u[2 * i + f : 2 * i + f + 1, :] = u_ref[at : at + 1, :]

    pl.semaphore_wait(barrier, events + 3)
    to_behind = pltpu.make_async_remote_copy(
        stage_g, ghost, halo_send.at[0], halo_recv.at[0], cut_at(-1), MESH
    )
    planes_ahead = pltpu.make_async_remote_copy(
        stage_u, tail_u, halo_send.at[1], halo_recv.at[1], cut_at(1), MESH
    )
    pl.when(jnp.logical_not(first))(to_behind.start)
    pl.when(final)(planes_ahead.start)

    twice = lambda x: jnp.concatenate([x, x], axis=0)
    kinds = (aym, aye, azm, aze)
    for c in (2, 0, 1):
        sums = [None] * 4
        for j in range(5):
            for k in range(5):
                at = 208 * c + 8 * (5 * j + k)
                moved = shifted(placed[at : at + 8, :], -(PZ * j + k))
                q = 2 * (j == 4) + (k == 4)
                sums[q] = moved if sums[q] is None else sums[q] + moved
        mm, me, em, ee = sums
        whole = (mm + me) + (em + ee)
        pairs = (mm + me, em + ee, mm + em, me + ee)
        if c == 2:
            ax[32:40, :] = twice(whole[0:4, :])
            for q in range(4):
                stage_a[4 + q : 5 + q, :] = sums[q][3:4, :]
                moved = pltpu.roll(twice(pairs[q][0:4, :]), 1, 0)
                kinds[q][0:8, :] = jnp.where(row % 4 == 0, 0.0, moved)
        else:
            for half in range(2):
                i = 2 * c + half
                some = slice(4 * half, 4 * half + 4)
                ax[8 * i : 8 * i + 8, :] = twice(whole[some, :])
                stage_a[i : i + 1, :] = whole[4 * half + 3 : 4 * half + 4, :]
                for q in range(4):
                    value = twice(pairs[q][some, :])
                    if i == 0:
                        value = value + kinds[q][0:8, :]
                    kinds[q][8 * i : 8 * i + 8, :] = value

    flux_ahead = pltpu.make_async_remote_copy(
        stage_a, tail_a, halo_send.at[2], halo_recv.at[2], cut_at(1), MESH
    )
    pl.when(final)(flux_ahead.start)

    loads[4].wait()
    axes = ((0, PZ, aym, aye), (8, 1, azm, aze))
    for i in range(4):
        at = 8 * i
        u = u_ref[at : at + 8, :]
        ksum = tsum = None
        for base, stride, m_ref, e_ref in axes:
            gm, ge = stencil(u, coef_ref, base, stride)
            fm, fe = m_ref[at : at + 8, :] * gm, e_ref[at : at + 8, :] * ge
            term = fm * pltpu.roll(gm, 4, 0) + fe * pltpu.roll(ge, 4, 0)
            ksum = term if ksum is None else ksum + term
            term = spread(fm, fe, coef_ref, base, stride)
            tsum = term if tsum is None else tsum + term
        kern[at : at + 8, :] = ksum
        force[at : at + 8, :] = tsum

    slab = [u_ref[8 * i : 8 * i + 8, :] for i in range(4)]
    slab.append(pltpu.roll(slab[0], 7, 0))
    grads = []
    for a in range(5):
        total = None
        for b in range(5):
            term = D[a][b] * slab[b]
            total = term if total is None else total + term
        grads.append(total)
    moved = [ax[8 * a : 8 * a + 8, :] * grads[a] for a in range(5)]
    prods = [moved[a] * pltpu.roll(grads[a], 4, 0) for a in range(5)]
    inner = row % 4 < 3
    after_first = row % 4 > 0
    terms = [kern[8 * i : 8 * i + 8, :] + jnp.where(inner, prods[i], 0.0) for i in range(4)]
    terms[0] = terms[0] + jnp.where(after_first, pltpu.roll(prods[4], 1, 0), 0.0)
    for half in range(2):
        nodes = jnp.where(row < 4, terms[2 * half], terms[2 * half + 1])
        for m in range(events + 1):
            part[m, 8 * half : 8 * half + 8, :] = nodes[:, 128 * m : 128 * m + 128]
    for m in range(events + 1):
        part[m, 16:24, :] = jnp.zeros((8, 128), f32)
    turned = []
    for a in range(5):
        total = None
        for b in range(5):
            term = D[b][a] * moved[b]
            total = term if total is None else total + term
        turned.append(jnp.where(inner, total, 0.0))
    turned[0] = turned[0] + jnp.where(after_first, pltpu.roll(turned[4], 1, 0), 0.0)
    for i in range(4):
        force[8 * i : 8 * i + 8, :] += turned[i]
    def slopes_of(plane):
        return [stencil(plane, coef_ref, base, stride) for base, stride, _, _ in axes]

    def last_layer(planes_ref, flux_ref, plane, slopes=None):
        edge = [planes_ref[2 * i : 2 * i + 2, :] for i in range(4)] + [plane]
        mm, me, em, ee = (flux_ref[4 + q : 5 + q, :] for q in range(4))
        edge_flux = [flux_ref[i : i + 1, :] for i in range(4)] + [(mm + me) + (em + ee)]
        grads = []
        for a in range(5):
            total = None
            for b in range(5):
                term = D[a][b] * edge[b]
                total = term if total is None else total + term
            grads.append(total)
        moved = [edge_flux[a] * grads[a] for a in range(5)]
        across = []
        for (gm, ge), am, ae in zip(slopes or slopes_of(plane), (mm + me, mm + em), (em + ee, me + ee)):
            across.append((gm, ge, am * gm, ae * ge))
        return grads, moved, across

    def last_terms(planes_ref, flux_ref, plane, slopes=None):
        grads, moved, across = last_layer(planes_ref, flux_ref, plane, slopes)
        terms = [moved[a][0:1, :] * grads[a][1:2, :] for a in range(5)]
        for gm, ge, fm, fe in across:
            terms[4] = terms[4] + fm[0:1, :] * gm[1:2, :] + fe[0:1, :] * ge[1:2, :]
        return terms

    def last_force(planes_ref, flux_ref, plane):
        _, moved, across = last_layer(planes_ref, flux_ref, plane)
        turned = []
        for a in range(5):
            total = None
            for b in range(5):
                term = D[b][a] * moved[b]
                total = term if total is None else total + term
            turned.append(total)
        for (base, stride, _, _), (_, _, fm, fe) in zip(axes, across):
            turned[4] = turned[4] + spread(fm, fe, coef_ref, base, stride)
        return turned

    @pl.when(jnp.logical_not(final))
    def _():
        to_behind.wait_recv()
        terms = last_terms(stage_u, stage_a, ghost[...])
        for m in range(events + 1):
            lanes = slice(128 * m, 128 * m + 128)
            for i in range(4):
                part[m, 4 * i + 3 : 4 * i + 4, :] += terms[i][:, lanes]
            part[m, 20:21, :] = terms[4][:, lanes]

    @pl.when(first)
    def _():
        plane = stage_g[...]
        slopes = slopes_of(plane)
        planes_ahead.wait_recv()
        flux_ahead.wait_recv()
        terms = last_terms(tail_u, tail_a, plane, slopes)
        for m in range(events + 1):
            lanes = slice(128 * m, 128 * m + 128)
            part[m, 0:1, :] += terms[4][:, lanes]
            for i in range(4):
                part[m, 16 + i : 17 + i, :] = terms[i][:, lanes]

    lead = e == events - 1
    for m in range(1, events):
        to = event_at(m)
        pltpu.make_async_remote_copy(
            part.at[to["event"]], recv.at[e], part_send, part_recv, to, MESH
        ).start()
    short_part = pltpu.make_async_remote_copy(
        part.at[events], recv_short.at[e], short_send, short_recv, {"event": events - 1}, MESH
    )
    pl.when(jnp.logical_not(lead))(short_part.start)
    recv[e] = part[e]

    force_ahead = pltpu.make_async_remote_copy(
        stage_f, carried, halo_send.at[3], halo_recv.at[3], cut_at(1), MESH
    )
    force_back = pltpu.make_async_remote_copy(
        stage_r, returned, halo_send.at[4], halo_recv.at[4], cut_at(-1), MESH
    )

    @pl.when(jnp.logical_not(final))
    def _():
        turned = last_force(stage_u, stage_a, ghost[...])
        stage_f[...] = turned[4]
        force_ahead.start()
        for i in range(4):
            for f in range(2):
                at = 8 * i + 4 * f + 3
                force[at : at + 1, :] += turned[i][f : f + 1, :]

    @pl.when(first)
    def _():
        turned = last_force(tail_u, tail_a, stage_g[...])
        for i in range(4):
            stage_r[2 * i : 2 * i + 2, :] = turned[i]
        force_back.start()
        for f in range(2):
            force[4 * f : 4 * f + 1, :] += turned[4][f : f + 1, :]

    for n in range(5, 9):
        loads[n].wait()

    def edges_of(n):
        return [
            pltpu.make_async_remote_copy(src, dst, edge_send.at[n, c], edge_recv.at[n, c], cut_at(m), MESH)
            for c, (src, dst, m) in enumerate(
                (
                    (total_ref.at[n], halo.at[n, 0], 1),
                    (total_ref.at[n], halo.at[n, 1], -1),
                    (total_ref.at[n, pl.ds(16, 8)], halo_far.at[n, 0], 2),
                    (total_ref.at[n, pl.ds(16, 8)], halo_far.at[n, 1], -2),
                )
            )
        ]

    def gathered(source, semaphore, n):
        some = source.at[pl.ds(0, events - 1)]
        pltpu.make_async_copy(some, some, semaphore).wait()
        total = source[0]
        for m in range(1, events):
            total = total + source[m]
        total_ref[n] = total
        for copy in edges_of(n):
            copy.start()

    def smoothed(n):
        for copy in edges_of(n):
            copy.wait_recv()
        parts = [halo[n, 0], total_ref[n], halo[n, 1]]
        tall = jnp.concatenate(
            [x[0:16, :] for x in parts] + [halo_far[n, 0]] + [x[16:24, :] for x in parts] + [halo_far[n, 1]],
            axis=0,
        )
        return jnp.dot(
            band_ref[:, 0:88], tall, precision=lax.Precision.HIGHEST, preferred_element_type=f32
        )

    gathered(recv, part_recv, 0)

    @pl.when(lead)
    def _():
        recv_short[e] = part[events]
        gathered(recv_short, short_recv, 1)

    cols[e] = smoothed(0)
    for m in range(1, events):
        pltpu.make_async_remote_copy(cols.at[e], cols.at[e], cols_send, cols_recv, event_at(m), MESH).start()
    shorts = [
        pltpu.make_async_remote_copy(lone, lone, lone_send.at[m], lone_recv, {"event": m}, MESH)
        for m in range(events - 1)
    ]

    @pl.when(lead)
    def _():
        lone[...] = smoothed(1)
        for copy in shorts:
            copy.start()

    @pl.when(jnp.logical_not(first))
    def _():
        force_ahead.wait_recv()
        for f in range(2):
            force[4 * f : 4 * f + 1, :] += carried[f : f + 1, :]

    @pl.when(final)
    def _():
        force_back.wait_recv()
        for i in range(4):
            for f in range(2):
                at = 8 * i + 4 * f + 3
                force[at : at + 1, :] += returned[2 * i + f : 2 * i + f + 1, :]

    ends = planes_to_flat(
        [force[8 * i : 8 * i + 8, :] for i in range(4)], (rows_a, rows_b), lane1, row1
    )
    for f, (sign, now_out, speed_out) in enumerate(
        ((time_step, fdn_ref, fvn_ref), (-time_step, adn_ref, avn_ref))
    ):
        rows = (rows_a, rows_b)[f]
        for g in range(18):
            at, size = 1024 * g, 1024 if g < 17 else 16
            push = rows[8 * g : 8 * g + 8, :].reshape(1, 1024) if g < 17 else ends[f]
            mass = run_of(mass_flat, at, size).reshape(1, size)
            speed = flats[2 + f, 0:1, at : at + size] + (sign * mass) * push
            speed_out[0:1, at : at + size] = speed
            now_out[0:1, at : at + size] = flats[f, 0:1, at : at + size] - sign * speed
    some = cols.at[pl.ds(0, events - 1)]
    pltpu.make_async_copy(some, some, cols_recv).wait()
    pl.when(jnp.logical_not(lead))(shorts[0].wait_recv)
    total = jnp.concatenate([cols[m] for m in range(events)] + [lone[...]], axis=1)
    across = None
    for d in range(-cross_reach, cross_reach + 1):
        term = coef_ref[20 + d : 21 + d, :] * shifted(total, PZ * d)
        across = term if across is None else across + term
    total, across = across, None
    for d in range(-cross_reach, cross_reach + 1):
        term = coef_ref[29 + d : 30 + d, :] * shifted(total, d)
        across = term if across is None else across + term
    sk_ref[...] = across[:, 0:PYZ]
    pltpu.make_async_copy(some, some, cols_send).wait()
    seven = recv.at[pl.ds(0, events - 1)]
    pltpu.make_async_copy(seven, seven, part_send).wait()
    for copy in edges_of(0):
        copy.wait_send()

    @pl.when(lead)
    def _():
        for copy in edges_of(1) + shorts:
            copy.wait_send()

    pl.when(jnp.logical_not(lead))(short_part.wait_send)
    pl.when(jnp.logical_not(first))(to_behind.wait_send)
    pl.when(jnp.logical_not(final))(force_ahead.wait_send)
    pl.when(first)(force_back.wait_send)

    @pl.when(final)
    def _():
        planes_ahead.wait_send()
        flux_ahead.wait_send()


def store_kernel(a, b, c, d, k, a_hbm, b_hbm, c_hbm, d_hbm, k_hbm, sem):
    pairs = ((k, k_hbm), (a, a_hbm), (b, b_hbm), (c, c_hbm), (d, d_hbm))
    copies = [pltpu.make_async_copy(src, dst, sem.at[n]) for n, (src, dst) in enumerate(pairs)]
    for copy in copies:
        copy.start()
    for copy in copies:
        copy.wait()


def on_device(events, slices):
    def run(fd, fv, ad, av, inverse_mass, shear, connectivity, face_points, count):
        vmem = pl.BlockSpec(memory_space=pltpu.VMEM)
        there = pl.BlockSpec(memory_space=pltpu.HBM)
        stay = lambda x: pltpu.with_memory_space_constraint(x, pltpu.HBM)
        f32 = jnp.float32
        flat = jax.ShapeDtypeStruct((1, NPTS), f32)
        table = jax.ShapeDtypeStruct((PXU, PYZ), f32)
        big = lambda *dims: pltpu.VMEM((*dims, LANES), f32)
        small = lambda *dims: pltpu.VMEM((*dims, 128), f32)
        dma = pltpu.SemaphoreType.DMA
        outs = pl.pallas_call(
            functools.partial(step_kernel, events, slices),
            out_shape=(flat, flat, flat, flat, table),
            in_specs=[there] * 7 + [pl.BlockSpec(memory_space=pltpu.SMEM)] + [there] * 2,
            out_specs=(vmem,) * 5,
            scratch_shapes=[
                pltpu.VMEM((4, 1, NPTS), f32),
                pltpu.VMEM((NPTS,), f32),
                small(280),
                small(8),
                small(136),
                small(136),
                pltpu.VMEM((125, 256), f32),
                pltpu.VMEM((8, 256), jnp.int32),
                big(56),
                small(16),
                big(32),
                pltpu.VMEM((2, 624, 256), jnp.bfloat16),
                big(624),
                big(40),
                big(32),
                big(32),
                big(32),
                big(32),
                big(2),
                big(8),
                big(2),
                big(8),
                big(8),
                big(2),
                big(2),
                big(8),
                big(8),
                big(8),
                big(32),
                big(32),
                small(events + 1, 24),
                small(events, 24),
                small(events, 24),
                small(2, 24),
                small(2, 2, 24),
                small(2, 2, 8),
                small(events, 16),
                small(16),
                dma((9,)),
                dma((5,)),
                dma((5,)),
                dma,
                dma,
                dma,
                dma,
                dma((2, 4)),
                dma((2, 4)),
                dma,
                dma,
                dma((events - 1,)),
                dma,
            ],
            compiler_params=pltpu.CompilerParams(
                collective_id=0, has_side_effects=True, vmem_limit_bytes=40 << 20
            ),
        )(
            *map(stay, (fd, fv, ad, av, inverse_mass, shear, connectivity)),
            count,
            stay(jnp.asarray(lane_tables())),
            stay(jnp.asarray(band_table())),
        )
        fdn, fvn, adn, avn, sk = pl.pallas_call(
            store_kernel,
            out_shape=(flat, flat, flat, flat, table),
            in_specs=[vmem] * 5,
            out_specs=(there,) * 5,
            scratch_shapes=[dma((5,))],
            compiler_params=pltpu.CompilerParams(vmem_limit_bytes=4 << 20),
        )(*outs)
        return fdn, fvn, adn, avn, sk

    return run


def solution(mesh):
    both = P("event", "cuts")
    return jax.shard_map(
        on_device(mesh.shape["event"], mesh.shape["cuts"]),
        mesh=mesh,
        in_specs=(
            both,
            both,
            both,
            both,
            P("cuts"),
            P(None, "cuts"),
            P(None, "cuts"),
            P("cuts", None),
            P("cuts"),
        ),
        out_specs=(both, both, both, both, P("cuts", None)),
        check_vma=False,
    )
```

```python
import functools

import jax
import jax.numpy as jnp
import numpy as np
from jax import lax
from jax.experimental import pallas as pl
from jax.experimental.pallas import tpu as pltpu
from jax.sharding import PartitionSpec as P

NGLL = 5
PXU = 16
PY = 33
PZ = 33
PYZ = 1089
NPTS = 17424
LANES = 1152

time_step = 0.02
cross_sigma = 1.5
cross_reach = 4

MESH = pl.DeviceIdType.MESH


def gll_tables():
    nodes = np.array([-1.0, -np.sqrt(3.0 / 7.0), 0.0, np.sqrt(3.0 / 7.0), 1.0])
    quad = np.array([0.1, 49.0 / 90.0, 32.0 / 45.0, 49.0 / 90.0, 0.1])
    bary = np.array(
        [1.0 / np.prod([nodes[a] - nodes[b] for b in range(5) if b != a]) for a in range(5)]
    )
    deriv = np.zeros((5, 5))
    for a in range(5):
        for b in range(5):
            if b != a:
                deriv[a, b] = bary[b] / bary[a] / (nodes[a] - nodes[b])
        deriv[a, a] = -np.sum(deriv[a])
    cube = (quad[:, None, None] * quad[None, :, None] * quad[None, None, :]).reshape(125)
    return deriv.astype(np.float32), cube.astype(np.float32)


DERIV, CUBE = gll_tables()
D = [[float(DERIV[a, b]) for b in range(5)] for a in range(5)]


def lane_tables():
    lane = np.arange(LANES)
    live = lane < PYZ
    y, z = lane // PZ, lane % PZ
    rows = []
    for pos, extent in ((y, PY), (z, PZ)):
        for d in range(-3, 5):
            node = pos % 4
            inside = live & (pos < extent - 1) & (node + d >= 0) & (node + d <= 4)
            value = DERIV[node, np.clip(node + d, 0, 4)]
            rows.append(np.where(inside, value, 0.0))
    for pos, extent in ((y, PY), (z, PZ)):
        weight = lambda d: np.exp(-d * d / (2.0 * cross_sigma * cross_sigma))
        norm = np.zeros(LANES)
        for d in range(-cross_reach, cross_reach + 1):
            norm += np.where((pos + d >= 0) & (pos + d < extent), weight(d), 0.0)
        for d in range(-cross_reach, cross_reach + 1):
            inside = live & (pos + d >= 0) & (pos + d < extent)
            rows.append(np.where(inside, weight(d) / norm, 0.0))
    rows = np.stack(rows).astype(np.float32)
    return np.pad(rows, ((0, 56 - rows.shape[0]), (0, 0)))


def band_table():
    sigma = PXU / 4.0
    w = lambda d: np.exp(-d * d / (2.0 * sigma * sigma))
    norm = np.sum(w(np.arange(-PXU, PXU + 1).astype(np.float64)))

    def table(places):
        gap = places[None, :] - np.arange(PXU)[:, None]
        return np.where(np.abs(gap) <= PXU, w(gap.astype(np.float64)) / norm, 0.0)

    rows = table(np.arange(-PXU, 2 * PXU)).reshape(PXU, 3, 4, 4).transpose(0, 1, 3, 2).reshape(PXU, 48)
    places = PXU * np.arange(-2, 3)[:, None] + np.array([-4, -3, -2, -1, 16])[None, :]
    extra = np.pad(table(places.reshape(25)).reshape(PXU, 5, 5), ((0, 0), (0, 0), (0, 3)))
    wrapped = table((np.array([-4, -20, 12, 28])[:, None] + np.arange(5)[None, :]).reshape(20))
    both = np.concatenate([rows, extra.reshape(PXU, 40), wrapped], axis=1)
    return np.pad(-both, ((0, 0), (0, 20))).astype(np.float32)


def shifted(x, step):
    shift = (-step) % LANES
    return x if shift == 0 else pltpu.roll(x, shift, 1)


def stencil(u, coef_ref, base, stride):
    main = end = None
    for d in range(-4, 5):
        moved = shifted(u, stride * d)
        if d >= -3:
            row = base + d + 3
            term = coef_ref[row : row + 1, :] * moved
            main = term if main is None else main + term
        if d <= 0:
            term = D[4][4 + d] * moved
            end = term if end is None else end + term
    return main, end


def spread(fm, fe, coef_ref, base, stride):
    total = None
    for d in range(-4, 5):
        term = None
        if d >= -3:
            row = base + d + 3
            term = coef_ref[row : row + 1, :] * fm
        if d <= 0:
            part = D[4][4 + d] * fe
            term = part if term is None else term + part
        term = shifted(term, -stride * d)
        total = term if total is None else total + term
    return total


FIRST = [PYZ * i // 128 for i in range(4)]
LEAD = [PYZ * i % 128 for i in range(4)]
GROUP = 34


def lane_starts(i, lane_row):
    return LEAD[i] + 4 * (lane_row % 4)


def run_of(flat_ref, start, size):
    if len(flat_ref.shape) == 1:
        return flat_ref[start : start + size]
    return flat_ref[0:1, start : start + size]


def flat_to_rows(flat_ref, both, first):
    for g in range(17):
        both[first + 8 * g : first + 8 * g + 8, :] = run_of(flat_ref, 1024 * g, 1024).reshape(8, 128)


def planes(both, tail_row, i, lane, row):
    tiles = []
    for t in range(10):
        at = FIRST[i] + t
        tile = both[pl.ds(at, 8, stride=GROUP), :]
        if i == 3 and t == 9:
            tile = jnp.where(row == 3, tail_row, tile)
        if LEAD[i]:
            tile = pltpu.roll(tile, 128 - LEAD[i], 1)
        tile = jnp.where(row % 2 == 1, pltpu.roll(tile, 124, 1), tile)
        tiles.append(jnp.where(row % 4 >= 2, pltpu.roll(tile, 120, 1), tile))
    keep = lane < 128 - lane_starts(i, row)
    return jnp.concatenate([jnp.where(keep, tiles[t], tiles[t + 1]) for t in range(9)], axis=1)


def planes_to_flat(slabs, rows_refs, lane, row):
    before = None
    done = []
    for i in range(4):
        tiles = []
        for t in range(9):
            tile = slabs[i][:, 128 * t : 128 * t + 128]
            if LEAD[i]:
                tile = pltpu.roll(tile, LEAD[i], 1)
            tile = jnp.where(row % 2 == 1, pltpu.roll(tile, 4, 1), tile)
            tiles.append(jnp.where(row % 4 >= 2, pltpu.roll(tile, 8, 1), tile))
        start = lane < lane_starts(i, row)
        count = (FIRST + [GROUP])[i + 1] - FIRST[i]
        for t in range(count):
            low = tiles[t - 1] if t else before
            done.append(tiles[t] if low is None else jnp.where(start, low, tiles[t]))
        before = tiles[8] if count == 9 else jnp.where(start, tiles[7], tiles[8])
    done[0] = jnp.where(lane < lane_starts(0, row), pltpu.roll(before, 1, 0), done[0])
    for f in range(2):
        rows = rows_refs[f]
        for g in range(GROUP):
            rows[pl.ds(g, 4, stride=GROUP), :] = done[g][4 * f : 4 * f + 4, :]
    return [before[4 * f + 3 : 4 * f + 4, 0:16] for f in range(2)]


def step_kernel(
    events,
    slices,
    fd_hbm,
    fv_hbm,
    ad_hbm,
    av_hbm,
    mass_hbm,
    shear_hbm,
    conn_hbm,
    count_ref,
    coef_hbm,
    band_hbm,
    fdn_ref,
    fvn_ref,
    adn_ref,
    avn_ref,
    sk_ref,
    flats,
    mass_flat,
    both,
    tails,
    rows_a,
    rows_b,
    shear_ref,
    conn_ref,
    coef_ref,
    band_ref,
    u_ref,
    lhs,
    placed,
    ax,
    aym,
    aye,
    azm,
    aze,
    carried,
    returned,
    ghost,
    tail_u,
    tail_a,
    stage_g,
    stage_f,
    stage_r,
    stage_u,
    stage_a,
    force,
    kern,
    part,
    recv,
    recv_short,
    total_ref,
    halo,
    halo_far,
    cols,
    lone,
    wrap_rows,
    wrap_extra,
    wrap_terms,
    wrap_total,
    wrap_near,
    wrap_sum,
    load_sem,
    halo_send,
    halo_recv,
    part_send,
    part_recv,
    short_send,
    short_recv,
    edge_send,
    edge_recv,
    cols_send,
    cols_recv,
    lone_send,
    lone_recv,
    ready,
    tile_send,
    tile_recv,
    extra_send,
    extra_recv,
    terms_send,
    terms_recv,
    near_send,
    near_recv,
):
    f32 = jnp.float32
    e = lax.axis_index("event")
    s = lax.axis_index("cuts")
    first, final = s == 0, s == slices - 1
    second, before_final = s == 1, s == slices - 2
    cut_at = lambda m: {"cuts": lax.rem(s + m + slices, slices)}

    barrier = pltpu.get_barrier_semaphore()

    def greet_cut(m):
        pl.semaphore_signal(barrier, inc=1, device_id=cut_at(m), device_id_type=MESH)

    greet_cut(-1)
    greet_cut(-2)
    pl.when(jnp.logical_not(final))(lambda: greet_cut(1))
    pl.when(s < slices - 2)(lambda: greet_cut(2))

    def event_at(m):
        return {"event": lax.rem(e + m, events)}

    for m in range(1, events):
        pl.semaphore_signal(barrier, inc=1, device_id=event_at(m), device_id_type=MESH)

    def greet(cut):
        for m in range(1, events):
            to = {**event_at(m), "cuts": cut}
            pl.semaphore_signal(barrier, inc=1, device_id=to, device_id_type=MESH)

    @pl.when(first)
    def _():
        greet(slices - 1)
        greet(slices - 2)


    @pl.when(first)
    def _():
        for n in range(2):
            halo[n, 0] = jnp.zeros((24, 128), jnp.float32)

    @pl.when(s <= 1)
    def _():
        for n in range(2):
            halo_far[n, 0] = jnp.zeros((8, 128), jnp.float32)

    wrap_sum[...] = jnp.zeros((PXU, LANES), jnp.float32)

    loads = [
        pltpu.make_async_copy(src, dst, load_sem.at[n])
        for n, (src, dst) in enumerate(
            (
                (conn_hbm.at[pl.ds(0, 8), :], conn_ref),
                (shear_hbm, shear_ref),
                (fd_hbm, flats.at[0]),
                (ad_hbm, flats.at[1]),
                (coef_hbm, coef_ref),
                (fv_hbm, flats.at[2]),
                (av_hbm, flats.at[3]),
                (mass_hbm, mass_flat),
                (band_hbm, band_ref),
            )
        )
    ]
    for load in loads:
        load.start()

    row = lax.broadcasted_iota(jnp.int32, (8, LANES), 0)
    row1 = lax.broadcasted_iota(jnp.int32, (8, 128), 0)
    lane1 = lax.broadcasted_iota(jnp.int32, (8, 128), 1)

    def slabs_of(first, second):
        flat_to_rows(first, both, 0)
        flat_to_rows(second, both, 136)
        tails[...] = jnp.zeros((8, 128), f32)
        tails[0:1, 0:16] = run_of(first, 17408, 16).reshape(1, 16)
        both[272:280, :] = jnp.zeros((8, 128), f32)
        both[272:273, 0:16] = run_of(second, 17408, 16).reshape(1, 16)
        return [planes(both, tails[0:1, :], i, lane1, row1) for i in range(4)]

    for n in (0, 1):
        loads[n].wait()
    corner = conn_ref[0:1, :]
    layer = sum(jnp.where(corner >= 4 * PYZ * n, 1, 0) for n in (1, 2, 3))
    base = jnp.broadcast_to(corner - 4 * PYZ * layer, (128, 256)).T
    wide_row = lax.broadcasted_iota(jnp.int32, (8, 256), 0)
    slot = lax.broadcasted_iota(jnp.int32, (8, 256), 1)
    own = jnp.where((wide_row % 4 == layer) & (slot < count_ref[0]), 1.0, 0.0)

    def flux_rows(c, jk):
        if jk == 25:
            return jnp.zeros((8, 256), f32)
        near = 50 * c + jk
        value = float(CUBE[near]) * shear_ref[near : near + 1, :]
        if c < 2:
            far = near + 25
            value = jnp.where(wide_row < 4, value, float(CUBE[far]) * shear_ref[far : far + 1, :])
        else:
            value = jnp.where(wide_row < 4, value, 0.0)
        return value * own

    for c in range(3):
        for pair in range(13):
            value = jnp.concatenate([flux_rows(c, 2 * pair), flux_rows(c, 2 * pair + 1)], axis=0)
            at = 208 * c + 16 * pair
            hi = value.astype(jnp.bfloat16)
            lhs[0, at : at + 16, :] = hi
            lhs[1, at : at + 16, :] = (value - hi.astype(f32)).astype(jnp.bfloat16)
    lane_wide = lax.broadcasted_iota(jnp.int32, (256, 128), 1)
    pick = jnp.concatenate(
        [jnp.where(base == lane_wide + 128 * t, 1.0, 0.0).astype(jnp.bfloat16) for t in range(9)], axis=1
    )
    placed[...] = jnp.dot(lhs[0], pick, preferred_element_type=f32) + jnp.dot(
        lhs[1], pick, preferred_element_type=f32
    )

    loads[2].wait()
    loads[3].wait()
    for i, value in enumerate(slabs_of(flats.at[0], flats.at[1])):
        u_ref[8 * i : 8 * i + 8, :] = value
    for f in range(2):
        stage_g[f : f + 1, :] = u_ref[4 * f : 4 * f + 1, :]
        for i in range(4):
            at = 8 * i + 4 * f + 3
            stage_u[2 * i + f : 2 * i + f + 1, :] = u_ref[at : at + 1, :]

    more = (events - 1) * jnp.where(s >= slices - 2, 1, 0)
    fewer = 2 * jnp.where(first, 1, 0) + jnp.where(second, 1, 0)
    pl.semaphore_wait(barrier, events + 3 + more - fewer)

    def tell(m):
        pl.semaphore_signal(ready, inc=1, device_id=cut_at(m), device_id_type=MESH)

    pl.when(final)(lambda: tell(1))
    pl.when(s >= slices - 2)(lambda: tell(2))
    to_behind = pltpu.make_async_remote_copy(
        stage_g, ghost, halo_send.at[0], halo_recv.at[0], cut_at(-1), MESH
    )
    planes_ahead = pltpu.make_async_remote_copy(
        stage_u, tail_u, halo_send.at[1], halo_recv.at[1], cut_at(1), MESH
    )
    pl.when(jnp.logical_not(first))(to_behind.start)
    pl.when(final)(planes_ahead.start)

    twice = lambda x: jnp.concatenate([x, x], axis=0)
    kinds = (aym, aye, azm, aze)
    for c in (2, 0, 1):
        sums = [None] * 4
        for j in range(5):
            for k in range(5):
                at = 208 * c + 8 * (5 * j + k)
                moved = shifted(placed[at : at + 8, :], -(PZ * j + k))
                q = 2 * (j == 4) + (k == 4)
                sums[q] = moved if sums[q] is None else sums[q] + moved
        mm, me, em, ee = sums
        whole = (mm + me) + (em + ee)
        pairs = (mm + me, em + ee, mm + em, me + ee)
        if c == 2:
            ax[32:40, :] = twice(whole[0:4, :])
            for q in range(4):
                stage_a[4 + q : 5 + q, :] = sums[q][3:4, :]
                moved = pltpu.roll(twice(pairs[q][0:4, :]), 1, 0)
                kinds[q][0:8, :] = jnp.where(row % 4 == 0, 0.0, moved)
        else:
            for half in range(2):
                i = 2 * c + half
                some = slice(4 * half, 4 * half + 4)
                ax[8 * i : 8 * i + 8, :] = twice(whole[some, :])
                stage_a[i : i + 1, :] = whole[4 * half + 3 : 4 * half + 4, :]
                for q in range(4):
                    value = twice(pairs[q][some, :])
                    if i == 0:
                        value = value + kinds[q][0:8, :]
                    kinds[q][8 * i : 8 * i + 8, :] = value

    flux_ahead = pltpu.make_async_remote_copy(
        stage_a, tail_a, halo_send.at[2], halo_recv.at[2], cut_at(1), MESH
    )
    pl.when(final)(flux_ahead.start)

    loads[4].wait()
    axes = ((0, PZ, aym, aye), (8, 1, azm, aze))
    for i in range(4):
        at = 8 * i
        u = u_ref[at : at + 8, :]
        ksum = tsum = None
        for base, stride, m_ref, e_ref in axes:
            gm, ge = stencil(u, coef_ref, base, stride)
            fm, fe = m_ref[at : at + 8, :] * gm, e_ref[at : at + 8, :] * ge
            term = fm * pltpu.roll(gm, 4, 0) + fe * pltpu.roll(ge, 4, 0)
            ksum = term if ksum is None else ksum + term
            term = spread(fm, fe, coef_ref, base, stride)
            tsum = term if tsum is None else tsum + term
        kern[at : at + 8, :] = ksum
        force[at : at + 8, :] = tsum

    slab = [u_ref[8 * i : 8 * i + 8, :] for i in range(4)]
    slab.append(pltpu.roll(slab[0], 7, 0))
    grads = []
    for a in range(5):
        total = None
        for b in range(5):
            term = D[a][b] * slab[b]
            total = term if total is None else total + term
        grads.append(total)
    moved = [ax[8 * a : 8 * a + 8, :] * grads[a] for a in range(5)]
    prods = [moved[a] * pltpu.roll(grads[a], 4, 0) for a in range(5)]
    inner = row % 4 < 3
    after_first = row % 4 > 0
    terms = [kern[8 * i : 8 * i + 8, :] + jnp.where(inner, prods[i], 0.0) for i in range(4)]
    terms[0] = terms[0] + jnp.where(after_first, pltpu.roll(prods[4], 1, 0), 0.0)
    for half in range(2):
        nodes = jnp.where(row < 4, terms[2 * half], terms[2 * half + 1])
        for m in range(events + 1):
            part[m, 8 * half : 8 * half + 8, :] = nodes[:, 128 * m : 128 * m + 128]
    for m in range(events + 1):
        part[m, 16:24, :] = jnp.zeros((8, 128), f32)
    turned = []
    for a in range(5):
        total = None
        for b in range(5):
            term = D[b][a] * moved[b]
            total = term if total is None else total + term
        turned.append(jnp.where(inner, total, 0.0))
    turned[0] = turned[0] + jnp.where(after_first, pltpu.roll(turned[4], 1, 0), 0.0)
    for i in range(4):
        force[8 * i : 8 * i + 8, :] += turned[i]
    def slopes_of(plane):
        return [stencil(plane, coef_ref, base, stride) for base, stride, _, _ in axes]

    def last_layer(planes_ref, flux_ref, plane, slopes=None):
        edge = [planes_ref[2 * i : 2 * i + 2, :] for i in range(4)] + [plane]
        mm, me, em, ee = (flux_ref[4 + q : 5 + q, :] for q in range(4))
        edge_flux = [flux_ref[i : i + 1, :] for i in range(4)] + [(mm + me) + (em + ee)]
        grads = []
        for a in range(5):
            total = None
            for b in range(5):
                term = D[a][b] * edge[b]
                total = term if total is None else total + term
            grads.append(total)
        moved = [edge_flux[a] * grads[a] for a in range(5)]
        across = []
        for (gm, ge), am, ae in zip(slopes or slopes_of(plane), (mm + me, mm + em), (em + ee, me + ee)):
            across.append((gm, ge, am * gm, ae * ge))
        return grads, moved, across

    def last_terms(planes_ref, flux_ref, plane, slopes=None):
        grads, moved, across = last_layer(planes_ref, flux_ref, plane, slopes)
        terms = [moved[a][0:1, :] * grads[a][1:2, :] for a in range(5)]
        for gm, ge, fm, fe in across:
            terms[4] = terms[4] + fm[0:1, :] * gm[1:2, :] + fe[0:1, :] * ge[1:2, :]
        return terms

    def last_force(planes_ref, flux_ref, plane):
        _, moved, across = last_layer(planes_ref, flux_ref, plane)
        turned = []
        for a in range(5):
            total = None
            for b in range(5):
                term = D[b][a] * moved[b]
                total = term if total is None else total + term
            turned.append(total)
        for (base, stride, _, _), (_, _, fm, fe) in zip(axes, across):
            turned[4] = turned[4] + spread(fm, fe, coef_ref, base, stride)
        return turned

    @pl.when(jnp.logical_not(final))
    def _():
        to_behind.wait_recv()
        terms = last_terms(stage_u, stage_a, ghost[...])
        for m in range(events + 1):
            lanes = slice(128 * m, 128 * m + 128)
            for i in range(4):
                part[m, 4 * i + 3 : 4 * i + 4, :] += terms[i][:, lanes]
            part[m, 20:21, :] = terms[4][:, lanes]

    lead = e == events - 1
    for m in range(1, events):
        to = event_at(m)
        pltpu.make_async_remote_copy(
            part.at[to["event"]], recv.at[e], part_send, part_recv, to, MESH
        ).start()
    short_part = pltpu.make_async_remote_copy(
        part.at[events], recv_short.at[e], short_send, short_recv, {"event": events - 1}, MESH
    )
    pl.when(jnp.logical_not(lead))(short_part.start)
    recv[e] = part[e]

    force_ahead = pltpu.make_async_remote_copy(
        stage_f, carried, halo_send.at[3], halo_recv.at[3], cut_at(1), MESH
    )
    force_back = pltpu.make_async_remote_copy(
        stage_r, returned, halo_send.at[4], halo_recv.at[4], cut_at(-1), MESH
    )

    @pl.when(jnp.logical_not(final))
    def _():
        turned = last_force(stage_u, stage_a, ghost[...])
        stage_f[...] = turned[4]
        force_ahead.start()
        for i in range(4):
            for f in range(2):
                at = 8 * i + 4 * f + 3
                force[at : at + 1, :] += turned[i][f : f + 1, :]

    for n in range(5, 9):
        loads[n].wait()

    def edges_of(n):
        return [
            pltpu.make_async_remote_copy(src, dst, edge_send.at[n, c], edge_recv.at[n, c], cut_at(m), MESH)
            for c, (src, dst, m) in enumerate(
                (
                    (total_ref.at[n], halo.at[n, 0], 1),
                    (total_ref.at[n], halo.at[n, 1], -1),
                    (total_ref.at[n, pl.ds(16, 8)], halo_far.at[n, 0], 2),
                    (total_ref.at[n, pl.ds(16, 8)], halo_far.at[n, 1], -2),
                )
            )
        ]

    def slot(n):
        return e if n == 0 else events

    def tiles_of(n):
        return [
            pltpu.make_async_remote_copy(
                total_ref.at[n, pl.ds(0, 16)], wrap_rows.at[slot(n)], tile_send.at[n, m], tile_recv, {"event": m, "cuts": 0}, MESH
            )
            for m in range(events)
        ]

    def extras_of(n):
        return [
            pltpu.make_async_remote_copy(
                total_ref.at[n, pl.ds(16, 8)],
                wrap_extra.at[slot(n)],
                extra_send.at[n, m],
                extra_recv,
                {"event": m, "cuts": 0},
                MESH,
            )
            for m in range(events)
        ]

    def gathered(source, semaphore, n):
        some = source.at[pl.ds(0, events - 1)]
        pltpu.make_async_copy(some, some, semaphore).wait()
        total = source[0]
        for m in range(1, events):
            total = total + source[m]
        total_ref[n] = total
        ahead, behind, far_ahead, far_behind = edges_of(n)
        pl.when(final)(lambda: [copy.start() for copy in tiles_of(n)] and None)
        pl.when(before_final)(lambda: [copy.start() for copy in extras_of(n)] and None)
        pl.when(jnp.logical_not(final))(ahead.start)
        pl.when(s < slices - 2)(far_ahead.start)

    def smoothed(n):
        ahead, behind, far_ahead, far_behind = edges_of(n)
        behind.wait_recv()
        far_behind.wait_recv()
        pl.when(jnp.logical_not(first))(ahead.wait_recv)
        pl.when(s > 1)(far_ahead.wait_recv)
        parts = [halo[n, 0], total_ref[n], halo[n, 1]]
        tall = jnp.concatenate(
            [x[0:16, :] for x in parts] + [halo_far[n, 0]] + [x[16:24, :] for x in parts] + [halo_far[n, 1]],
            axis=0,
        )
        return jnp.dot(
            band_ref[:, 0:88], tall, precision=lax.Precision.HIGHEST, preferred_element_type=f32
        )

    def back_edges(n):
        _, behind, _, far_behind = edges_of(n)
        behind.start()
        far_behind.start()

    gathered(recv, part_recv, 0)

    @pl.when(lead)
    def _():
        recv_short[e] = part[events]
        gathered(recv_short, short_recv, 1)

    pl.when(first)(lambda: pl.semaphore_wait(ready, 2))
    pl.when(second)(lambda: pl.semaphore_wait(ready, 1))
    back_edges(0)
    pl.when(lead)(lambda: back_edges(1))

    cols[e] = smoothed(0)
    for m in range(1, events):
        pltpu.make_async_remote_copy(cols.at[e], cols.at[e], cols_send, cols_recv, event_at(m), MESH).start()
    shorts = [
        pltpu.make_async_remote_copy(lone, lone, lone_send.at[m], lone_recv, {"event": m}, MESH)
        for m in range(events - 1)
    ]

    @pl.when(lead)
    def _():
        lone[...] = smoothed(1)
        for copy in shorts:
            copy.start()

    @pl.when(first)
    def _():
        plane = stage_g[...]
        slopes = slopes_of(plane)
        planes_ahead.wait_recv()
        flux_ahead.wait_recv()
        terms = last_terms(tail_u, tail_a, plane, slopes)
        for i in range(5):
            wrap_terms[e, i : i + 1, :] = terms[i]
        for m in range(1, events):
            pltpu.make_async_remote_copy(
                wrap_terms.at[e], wrap_terms.at[e], terms_send, terms_recv, event_at(m), MESH
            ).start()

    @pl.when(first)
    def _():
        turned = last_force(tail_u, tail_a, stage_g[...])
        for i in range(4):
            stage_r[2 * i : 2 * i + 2, :] = turned[i]
        force_back.start()
        for f in range(2):
            force[4 * f : 4 * f + 1, :] += turned[4][f : f + 1, :]

    @pl.when(jnp.logical_not(first))
    def _():
        force_ahead.wait_recv()
        for f in range(2):
            force[4 * f : 4 * f + 1, :] += carried[f : f + 1, :]

    @pl.when(final)
    def _():
        force_back.wait_recv()
        for i in range(4):
            for f in range(2):
                at = 8 * i + 4 * f + 3
                force[at : at + 1, :] += returned[2 * i + f : 2 * i + f + 1, :]

    ends = planes_to_flat(
        [force[8 * i : 8 * i + 8, :] for i in range(4)], (rows_a, rows_b), lane1, row1
    )
    for f, (sign, now_out, speed_out) in enumerate(
        ((time_step, fdn_ref, fvn_ref), (-time_step, adn_ref, avn_ref))
    ):
        rows = (rows_a, rows_b)[f]
        for g in range(18):
            at, size = 1024 * g, 1024 if g < 17 else 16
            push = rows[8 * g : 8 * g + 8, :].reshape(1, 1024) if g < 17 else ends[f]
            mass = run_of(mass_flat, at, size).reshape(1, size)
            speed = flats[2 + f, 0:1, at : at + size] + (sign * mass) * push
            speed_out[0:1, at : at + size] = speed
            now_out[0:1, at : at + size] = flats[f, 0:1, at : at + size] - sign * speed
    nears = [
        pltpu.make_async_remote_copy(wrap_total, wrap_near, near_send.at[n], near_recv, cut_at(m), MESH)
        for n, m in enumerate((1, -1, -2))
    ]
    table = band_ref[...]

    def add(weights, rows):
        wrap_sum[...] += jnp.dot(
            weights, rows, precision=lax.Precision.HIGHEST, preferred_element_type=f32
        )

    def wide(ref, start, size):
        return jnp.concatenate([ref[m, start : start + size, :] for m in range(events + 1)], axis=1)

    @pl.when(first)
    def _():
        seven = wrap_terms.at[pl.ds(0, events - 1)]
        pltpu.make_async_copy(seven, seven, terms_recv).wait()
        total = wrap_terms[0]
        for m in range(1, events):
            total = total + wrap_terms[m]
        wrap_total[...] = total
        for copy in nears:
            copy.start()
        pltpu.make_async_copy(wrap_rows, wrap_rows, tile_recv).wait()
        pltpu.make_async_copy(wrap_extra, wrap_extra, extra_recv).wait()
        add(table[:, 88:93], total)
        weights = jnp.concatenate([table[:, 0:16], table[:, 48:56]], axis=1)
        add(weights, jnp.concatenate([wide(wrap_rows, 0, 16), wide(wrap_extra, 0, 8)], axis=0))

    for n, place in enumerate((second, final, before_final)):
        @pl.when(place)
        def _():
            nears[0].wait_recv()
            add(table[:, 93 + 5 * n : 98 + 5 * n], wrap_near[...])

    some = cols.at[pl.ds(0, events - 1)]
    pltpu.make_async_copy(some, some, cols_recv).wait()
    pl.when(jnp.logical_not(lead))(shorts[0].wait_recv)
    total = jnp.concatenate([cols[m] for m in range(events)] + [lone[...]], axis=1) + wrap_sum[...]
    across = None
    for d in range(-cross_reach, cross_reach + 1):
        term = coef_ref[20 + d : 21 + d, :] * shifted(total, PZ * d)
        across = term if across is None else across + term
    total, across = across, None
    for d in range(-cross_reach, cross_reach + 1):
        term = coef_ref[29 + d : 30 + d, :] * shifted(total, d)
        across = term if across is None else across + term
    sk_ref[...] = across[:, 0:PYZ]
    pltpu.make_async_copy(some, some, cols_send).wait()
    seven = recv.at[pl.ds(0, events - 1)]
    pltpu.make_async_copy(seven, seven, part_send).wait()

    def sent(n):
        ahead, behind, far_ahead, far_behind = edges_of(n)
        behind.wait_send()
        far_behind.wait_send()
        pl.when(jnp.logical_not(final))(ahead.wait_send)
        pl.when(s < slices - 2)(far_ahead.wait_send)
        pl.when(final)(lambda: [copy.wait_send() for copy in tiles_of(n)] and None)
        pl.when(before_final)(lambda: [copy.wait_send() for copy in extras_of(n)] and None)

    sent(0)

    @pl.when(lead)
    def _():
        sent(1)
        for copy in shorts:
            copy.wait_send()

    @pl.when(first)
    def _():
        seven = wrap_terms.at[pl.ds(0, events - 1)]
        pltpu.make_async_copy(seven, seven, terms_send).wait()
        for copy in nears:
            copy.wait_send()

    pl.when(jnp.logical_not(lead))(short_part.wait_send)
    pl.when(jnp.logical_not(first))(to_behind.wait_send)
    pl.when(jnp.logical_not(final))(force_ahead.wait_send)
    pl.when(first)(force_back.wait_send)

    @pl.when(final)
    def _():
        planes_ahead.wait_send()
        flux_ahead.wait_send()


def store_kernel(a, b, c, d, k, a_hbm, b_hbm, c_hbm, d_hbm, k_hbm, sem):
    pairs = ((k, k_hbm), (a, a_hbm), (b, b_hbm), (c, c_hbm), (d, d_hbm))
    copies = [pltpu.make_async_copy(src, dst, sem.at[n]) for n, (src, dst) in enumerate(pairs)]
    for copy in copies:
        copy.start()
    for copy in copies:
        copy.wait()


def on_device(events, slices):
    def run(fd, fv, ad, av, inverse_mass, shear, connectivity, face_points, count):
        vmem = pl.BlockSpec(memory_space=pltpu.VMEM)
        there = pl.BlockSpec(memory_space=pltpu.HBM)
        stay = lambda x: pltpu.with_memory_space_constraint(x, pltpu.HBM)
        f32 = jnp.float32
        flat = jax.ShapeDtypeStruct((1, NPTS), f32)
        table = jax.ShapeDtypeStruct((PXU, PYZ), f32)
        big = lambda *dims: pltpu.VMEM((*dims, LANES), f32)
        small = lambda *dims: pltpu.VMEM((*dims, 128), f32)
        dma = pltpu.SemaphoreType.DMA
        outs = pl.pallas_call(
            functools.partial(step_kernel, events, slices),
            out_shape=(flat, flat, flat, flat, table),
            in_specs=[there] * 7 + [pl.BlockSpec(memory_space=pltpu.SMEM)] + [there] * 2,
            out_specs=(vmem,) * 5,
            scratch_shapes=[
                pltpu.VMEM((4, 1, NPTS), f32),
                pltpu.VMEM((NPTS,), f32),
                small(280),
                small(8),
                small(136),
                small(136),
                pltpu.VMEM((125, 256), f32),
                pltpu.VMEM((8, 256), jnp.int32),
                big(56),
                small(16),
                big(32),
                pltpu.VMEM((2, 624, 256), jnp.bfloat16),
                big(624),
                big(40),
                big(32),
                big(32),
                big(32),
                big(32),
                big(2),
                big(8),
                big(2),
                big(8),
                big(8),
                big(2),
                big(2),
                big(8),
                big(8),
                big(8),
                big(32),
                big(32),
                small(events + 1, 24),
                small(events, 24),
                small(events, 24),
                small(2, 24),
                small(2, 2, 24),
                small(2, 2, 8),
                small(events, 16),
                small(16),
                small(events + 1, 16),
                small(events + 1, 8),
                big(events, 5),
                big(5),
                big(5),
                big(16),
                dma((9,)),
                dma((5,)),
                dma((5,)),
                dma,
                dma,
                dma,
                dma,
                dma((2, 4)),
                dma((2, 4)),
                dma,
                dma,
                dma((events - 1,)),
                dma,
                pltpu.SemaphoreType.REGULAR,
                dma((2, events)),
                dma,
                dma((2, events)),
                dma,
                dma,
                dma,
                dma((3,)),
                dma,
            ],
            compiler_params=pltpu.CompilerParams(
                collective_id=0, has_side_effects=True, vmem_limit_bytes=40 << 20
            ),
        )(
            *map(stay, (fd, fv, ad, av, inverse_mass, shear, connectivity)),
            count,
            stay(jnp.asarray(lane_tables())),
            stay(jnp.asarray(band_table())),
        )
        fdn, fvn, adn, avn, sk = pl.pallas_call(
            store_kernel,
            out_shape=(flat, flat, flat, flat, table),
            in_specs=[vmem] * 5,
            out_specs=(there,) * 5,
            scratch_shapes=[dma((5,))],
            compiler_params=pltpu.CompilerParams(vmem_limit_bytes=4 << 20),
        )(*outs)
        return fdn, fvn, adn, avn, sk

    return run


def solution(mesh):
    both = P("event", "cuts")
    return jax.shard_map(
        on_device(mesh.shape["event"], mesh.shape["cuts"]),
        mesh=mesh,
        in_specs=(
            both,
            both,
            both,
            both,
            P("cuts"),
            P(None, "cuts"),
            P(None, "cuts"),
            P("cuts", None),
            P("cuts"),
        ),
        out_specs=(both, both, both, both, P("cuts", None)),
        check_vma=False,
    )
```

```python
import functools

import jax
import jax.numpy as jnp
import numpy as np
from jax import lax
from jax.experimental import pallas as pl
from jax.experimental.pallas import tpu as pltpu
from jax.sharding import PartitionSpec as P

NGLL = 5
PXU = 16
PY = 33
PZ = 33
PYZ = 1089
NPTS = 17424
LANES = 1152

time_step = 0.02
cross_sigma = 1.5
cross_reach = 4

MESH = pl.DeviceIdType.MESH


def gll_tables():
    nodes = np.array([-1.0, -np.sqrt(3.0 / 7.0), 0.0, np.sqrt(3.0 / 7.0), 1.0])
    quad = np.array([0.1, 49.0 / 90.0, 32.0 / 45.0, 49.0 / 90.0, 0.1])
    bary = np.array(
        [1.0 / np.prod([nodes[a] - nodes[b] for b in range(5) if b != a]) for a in range(5)]
    )
    deriv = np.zeros((5, 5))
    for a in range(5):
        for b in range(5):
            if b != a:
                deriv[a, b] = bary[b] / bary[a] / (nodes[a] - nodes[b])
        deriv[a, a] = -np.sum(deriv[a])
    cube = (quad[:, None, None] * quad[None, :, None] * quad[None, None, :]).reshape(125)
    return deriv.astype(np.float32), cube.astype(np.float32)


DERIV, CUBE = gll_tables()
D = [[float(DERIV[a, b]) for b in range(5)] for a in range(5)]


def lane_tables():
    lane = np.arange(LANES)
    live = lane < PYZ
    y, z = lane // PZ, lane % PZ
    rows = []
    for pos, extent in ((y, PY), (z, PZ)):
        for d in range(-3, 5):
            node = pos % 4
            inside = live & (pos < extent - 1) & (node + d >= 0) & (node + d <= 4)
            value = DERIV[node, np.clip(node + d, 0, 4)]
            rows.append(np.where(inside, value, 0.0))
    for pos, extent in ((y, PY), (z, PZ)):
        weight = lambda d: np.exp(-d * d / (2.0 * cross_sigma * cross_sigma))
        norm = np.zeros(LANES)
        for d in range(-cross_reach, cross_reach + 1):
            norm += np.where((pos + d >= 0) & (pos + d < extent), weight(d), 0.0)
        for d in range(-cross_reach, cross_reach + 1):
            inside = live & (pos + d >= 0) & (pos + d < extent)
            rows.append(np.where(inside, weight(d) / norm, 0.0))
    rows = np.stack(rows).astype(np.float32)
    return np.pad(rows, ((0, 56 - rows.shape[0]), (0, 0)))


def band_table():
    sigma = PXU / 4.0
    w = lambda d: np.exp(-d * d / (2.0 * sigma * sigma))
    norm = np.sum(w(np.arange(-PXU, PXU + 1).astype(np.float64)))

    def table(places):
        gap = places[None, :] - np.arange(PXU)[:, None]
        return np.where(np.abs(gap) <= PXU, w(gap.astype(np.float64)) / norm, 0.0)

    rows = table(np.arange(-PXU, 2 * PXU)).reshape(PXU, 3, 4, 4).transpose(0, 1, 3, 2).reshape(PXU, 48)
    places = PXU * np.arange(-2, 3)[:, None] + np.array([-4, -3, -2, -1, 16])[None, :]
    extra = np.pad(table(places.reshape(25)).reshape(PXU, 5, 5), ((0, 0), (0, 0), (0, 3)))
    wrapped = table((np.array([-4, -20, 12, 28])[:, None] + np.arange(5)[None, :]).reshape(20))
    both = np.concatenate([rows, extra.reshape(PXU, 40), wrapped], axis=1)
    return np.pad(-both, ((0, 0), (0, 20))).astype(np.float32)


def shifted(x, step):
    shift = (-step) % LANES
    return x if shift == 0 else pltpu.roll(x, shift, 1)


def stencil(u, coef_ref, base, stride):
    main = end = None
    for d in range(-4, 5):
        moved = shifted(u, stride * d)
        if d >= -3:
            row = base + d + 3
            term = coef_ref[row : row + 1, :] * moved
            main = term if main is None else main + term
        if d <= 0:
            term = D[4][4 + d] * moved
            end = term if end is None else end + term
    return main, end


def spread(fm, fe, coef_ref, base, stride):
    total = None
    for d in range(-4, 5):
        term = None
        if d >= -3:
            row = base + d + 3
            term = coef_ref[row : row + 1, :] * fm
        if d <= 0:
            part = D[4][4 + d] * fe
            term = part if term is None else term + part
        term = shifted(term, -stride * d)
        total = term if total is None else total + term
    return total


FIRST = [PYZ * i // 128 for i in range(4)]
LEAD = [PYZ * i % 128 for i in range(4)]
GROUP = 34


def lane_starts(i, lane_row):
    return LEAD[i] + 4 * (lane_row % 4)


def run_of(flat_ref, start, size):
    if len(flat_ref.shape) == 1:
        return flat_ref[start : start + size]
    return flat_ref[0:1, start : start + size]


def flat_to_rows(flat_ref, both, first):
    for g in range(17):
        both[first + 8 * g : first + 8 * g + 8, :] = run_of(flat_ref, 1024 * g, 1024).reshape(8, 128)


def planes(both, tail_row, i, lane, row):
    tiles = []
    for t in range(10):
        at = FIRST[i] + t
        tile = both[pl.ds(at, 8, stride=GROUP), :]
        if i == 3 and t == 9:
            tile = jnp.where(row == 3, tail_row, tile)
        if LEAD[i]:
            tile = pltpu.roll(tile, 128 - LEAD[i], 1)
        tile = jnp.where(row % 2 == 1, pltpu.roll(tile, 124, 1), tile)
        tiles.append(jnp.where(row % 4 >= 2, pltpu.roll(tile, 120, 1), tile))
    keep = lane < 128 - lane_starts(i, row)
    return jnp.concatenate([jnp.where(keep, tiles[t], tiles[t + 1]) for t in range(9)], axis=1)


def planes_to_flat(slabs, rows_refs, lane, row):
    before = None
    done = []
    for i in range(4):
        tiles = []
        for t in range(9):
            tile = slabs[i][:, 128 * t : 128 * t + 128]
            if LEAD[i]:
                tile = pltpu.roll(tile, LEAD[i], 1)
            tile = jnp.where(row % 2 == 1, pltpu.roll(tile, 4, 1), tile)
            tiles.append(jnp.where(row % 4 >= 2, pltpu.roll(tile, 8, 1), tile))
        start = lane < lane_starts(i, row)
        count = (FIRST + [GROUP])[i + 1] - FIRST[i]
        for t in range(count):
            low = tiles[t - 1] if t else before
            done.append(tiles[t] if low is None else jnp.where(start, low, tiles[t]))
        before = tiles[8] if count == 9 else jnp.where(start, tiles[7], tiles[8])
    done[0] = jnp.where(lane < lane_starts(0, row), pltpu.roll(before, 1, 0), done[0])
    for f in range(2):
        rows = rows_refs[f]
        for g in range(GROUP):
            rows[pl.ds(g, 4, stride=GROUP), :] = done[g][4 * f : 4 * f + 4, :]
    return [before[4 * f + 3 : 4 * f + 4, 0:16] for f in range(2)]


def step_kernel(
    events,
    slices,
    fd_hbm,
    fv_hbm,
    ad_hbm,
    av_hbm,
    mass_hbm,
    shear_hbm,
    conn_hbm,
    count_ref,
    coef_hbm,
    band_hbm,
    fdn_ref,
    fvn_ref,
    adn_ref,
    avn_ref,
    sk_ref,
    flats,
    mass_flat,
    both,
    tails,
    rows_a,
    rows_b,
    shear_ref,
    conn_ref,
    coef_ref,
    band_ref,
    u_ref,
    lhs,
    placed,
    ax,
    aym,
    aye,
    azm,
    aze,
    carried,
    returned,
    ghost,
    tail_u,
    tail_a,
    stage_g,
    stage_f,
    stage_r,
    stage_u,
    stage_a,
    force,
    kern,
    part,
    recv,
    recv_short,
    total_ref,
    halo,
    halo_far,
    cols,
    wrap_rows,
    wrap_extra,
    wrap_terms,
    wrap_total,
    wrap_near,
    wrap_sum,
    load_sem,
    halo_send,
    halo_recv,
    part_send,
    part_recv,
    short_send,
    short_recv,
    edge_send,
    edge_recv,
    cols_send,
    cols_recv,
    lone_send,
    ready,
    tile_send,
    tile_recv,
    extra_send,
    extra_recv,
    terms_send,
    terms_recv,
    near_send,
    near_recv,
):
    f32 = jnp.float32
    e = lax.axis_index("event")
    s = lax.axis_index("cuts")
    first, final = s == 0, s == slices - 1
    second, before_final = s == 1, s == slices - 2
    cut_at = lambda m: {"cuts": lax.rem(s + m + slices, slices)}

    barrier = pltpu.get_barrier_semaphore()

    def greet_cut(m):
        pl.semaphore_signal(barrier, inc=1, device_id=cut_at(m), device_id_type=MESH)

    greet_cut(-1)
    greet_cut(-2)
    pl.when(jnp.logical_not(final))(lambda: greet_cut(1))
    pl.when(s < slices - 2)(lambda: greet_cut(2))

    def event_at(m):
        return {"event": lax.rem(e + m, events)}

    order = sorted(range(1, events), key=lambda m: abs(m - events // 2))
    for m in order:
        pl.semaphore_signal(barrier, inc=1, device_id=event_at(m), device_id_type=MESH)

    def greet(cut):
        for m in range(1, events):
            to = {**event_at(m), "cuts": cut}
            pl.semaphore_signal(barrier, inc=1, device_id=to, device_id_type=MESH)

    @pl.when(first)
    def _():
        greet(slices - 1)
        greet(slices - 2)


    @pl.when(first)
    def _():
        for n in range(2):
            halo[n, 0] = jnp.zeros((24, 128), jnp.float32)

    @pl.when(s <= 1)
    def _():
        for n in range(2):
            halo_far[n, 0] = jnp.zeros((8, 128), jnp.float32)

    wrap_sum[...] = jnp.zeros((PXU, LANES), jnp.float32)

    loads = [
        pltpu.make_async_copy(src, dst, load_sem.at[n])
        for n, (src, dst) in enumerate(
            (
                (conn_hbm.at[pl.ds(0, 8), :], conn_ref),
                (shear_hbm, shear_ref),
                (fd_hbm, flats.at[0]),
                (ad_hbm, flats.at[1]),
                (coef_hbm, coef_ref),
                (fv_hbm, flats.at[2]),
                (av_hbm, flats.at[3]),
                (mass_hbm, mass_flat),
                (band_hbm, band_ref),
            )
        )
    ]
    for load in loads:
        load.start()

    row = lax.broadcasted_iota(jnp.int32, (8, LANES), 0)
    row1 = lax.broadcasted_iota(jnp.int32, (8, 128), 0)
    lane1 = lax.broadcasted_iota(jnp.int32, (8, 128), 1)

    def slabs_of(first, second):
        flat_to_rows(first, both, 0)
        flat_to_rows(second, both, 136)
        tails[...] = jnp.zeros((8, 128), f32)
        tails[0:1, 0:16] = run_of(first, 17408, 16).reshape(1, 16)
        both[272:280, :] = jnp.zeros((8, 128), f32)
        both[272:273, 0:16] = run_of(second, 17408, 16).reshape(1, 16)
        return [planes(both, tails[0:1, :], i, lane1, row1) for i in range(4)]

    for n in (0, 1):
        loads[n].wait()
    corner = conn_ref[0:1, :]
    layer = sum(jnp.where(corner >= 4 * PYZ * n, 1, 0) for n in (1, 2, 3))
    base = jnp.broadcast_to(corner - 4 * PYZ * layer, (128, 256)).T
    wide_row = lax.broadcasted_iota(jnp.int32, (8, 256), 0)
    slot = lax.broadcasted_iota(jnp.int32, (8, 256), 1)
    own = jnp.where((wide_row % 4 == layer) & (slot < count_ref[0]), 1.0, 0.0)

    def flux_rows(c, jk):
        if jk == 25:
            return jnp.zeros((8, 256), f32)
        near = 50 * c + jk
        value = float(CUBE[near]) * shear_ref[near : near + 1, :]
        if c < 2:
            far = near + 25
            value = jnp.where(wide_row < 4, value, float(CUBE[far]) * shear_ref[far : far + 1, :])
        else:
            value = jnp.where(wide_row < 4, value, 0.0)
        return value * own

    for c in range(3):
        for pair in range(13):
            value = jnp.concatenate([flux_rows(c, 2 * pair), flux_rows(c, 2 * pair + 1)], axis=0)
            at = 208 * c + 16 * pair
            hi = value.astype(jnp.bfloat16)
            lhs[0, at : at + 16, :] = hi
            lhs[1, at : at + 16, :] = (value - hi.astype(f32)).astype(jnp.bfloat16)
    lane_wide = lax.broadcasted_iota(jnp.int32, (256, 128), 1)
    pick = jnp.concatenate(
        [jnp.where(base == lane_wide + 128 * t, 1.0, 0.0).astype(jnp.bfloat16) for t in range(9)], axis=1
    )
    placed[...] = jnp.dot(lhs[0], pick, preferred_element_type=f32) + jnp.dot(
        lhs[1], pick, preferred_element_type=f32
    )

    loads[2].wait()
    loads[3].wait()
    for i, value in enumerate(slabs_of(flats.at[0], flats.at[1])):
        u_ref[8 * i : 8 * i + 8, :] = value
    for f in range(2):
        stage_g[f : f + 1, :] = u_ref[4 * f : 4 * f + 1, :]
        for i in range(4):
            at = 8 * i + 4 * f + 3
            stage_u[2 * i + f : 2 * i + f + 1, :] = u_ref[at : at + 1, :]

    more = (events - 1) * jnp.where(s >= slices - 2, 1, 0)
    fewer = 2 * jnp.where(first, 1, 0) + jnp.where(second, 1, 0)
    pl.semaphore_wait(barrier, events + 3 + more - fewer)

    def tell(m):
        pl.semaphore_signal(ready, inc=1, device_id=cut_at(m), device_id_type=MESH)

    pl.when(final)(lambda: tell(1))
    pl.when(s >= slices - 2)(lambda: tell(2))
    to_behind = pltpu.make_async_remote_copy(
        stage_g, ghost, halo_send.at[0], halo_recv.at[0], cut_at(-1), MESH
    )
    planes_ahead = pltpu.make_async_remote_copy(
        stage_u, tail_u, halo_send.at[1], halo_recv.at[1], cut_at(1), MESH
    )
    pl.when(jnp.logical_not(first))(to_behind.start)
    pl.when(final)(planes_ahead.start)

    twice = lambda x: jnp.concatenate([x, x], axis=0)
    kinds = (aym, aye, azm, aze)
    for c in (2, 0, 1):
        sums = [None] * 4
        for j in range(5):
            for k in range(5):
                at = 208 * c + 8 * (5 * j + k)
                moved = shifted(placed[at : at + 8, :], -(PZ * j + k))
                q = 2 * (j == 4) + (k == 4)
                sums[q] = moved if sums[q] is None else sums[q] + moved
        mm, me, em, ee = sums
        whole = (mm + me) + (em + ee)
        pairs = (mm + me, em + ee, mm + em, me + ee)
        if c == 2:
            ax[32:40, :] = twice(whole[0:4, :])
            for q in range(4):
                stage_a[4 + q : 5 + q, :] = sums[q][3:4, :]
                moved = pltpu.roll(twice(pairs[q][0:4, :]), 1, 0)
                kinds[q][0:8, :] = jnp.where(row % 4 == 0, 0.0, moved)
        else:
            for half in range(2):
                i = 2 * c + half
                some = slice(4 * half, 4 * half + 4)
                ax[8 * i : 8 * i + 8, :] = twice(whole[some, :])
                stage_a[i : i + 1, :] = whole[4 * half + 3 : 4 * half + 4, :]
                for q in range(4):
                    value = twice(pairs[q][some, :])
                    if i == 0:
                        value = value + kinds[q][0:8, :]
                    kinds[q][8 * i : 8 * i + 8, :] = value

    flux_ahead = pltpu.make_async_remote_copy(
        stage_a, tail_a, halo_send.at[2], halo_recv.at[2], cut_at(1), MESH
    )
    pl.when(final)(flux_ahead.start)

    loads[4].wait()
    axes = ((0, PZ, aym, aye), (8, 1, azm, aze))
    for i in range(4):
        at = 8 * i
        u = u_ref[at : at + 8, :]
        ksum = tsum = None
        for base, stride, m_ref, e_ref in axes:
            gm, ge = stencil(u, coef_ref, base, stride)
            fm, fe = m_ref[at : at + 8, :] * gm, e_ref[at : at + 8, :] * ge
            term = fm * pltpu.roll(gm, 4, 0) + fe * pltpu.roll(ge, 4, 0)
            ksum = term if ksum is None else ksum + term
            term = spread(fm, fe, coef_ref, base, stride)
            tsum = term if tsum is None else tsum + term
        kern[at : at + 8, :] = ksum
        force[at : at + 8, :] = tsum

    slab = [u_ref[8 * i : 8 * i + 8, :] for i in range(4)]
    slab.append(pltpu.roll(slab[0], 7, 0))
    grads = []
    for a in range(5):
        total = None
        for b in range(5):
            term = D[a][b] * slab[b]
            total = term if total is None else total + term
        grads.append(total)
    moved = [ax[8 * a : 8 * a + 8, :] * grads[a] for a in range(5)]
    prods = [moved[a] * pltpu.roll(grads[a], 4, 0) for a in range(5)]
    inner = row % 4 < 3
    after_first = row % 4 > 0
    terms = [kern[8 * i : 8 * i + 8, :] + jnp.where(inner, prods[i], 0.0) for i in range(4)]
    terms[0] = terms[0] + jnp.where(after_first, pltpu.roll(prods[4], 1, 0), 0.0)
    for half in range(2):
        nodes = jnp.where(row < 4, terms[2 * half], terms[2 * half + 1])
        for m in range(events + 1):
            part[m, 8 * half : 8 * half + 8, :] = nodes[:, 128 * m : 128 * m + 128]
    for m in range(events + 1):
        part[m, 16:24, :] = jnp.zeros((8, 128), f32)
    turned = []
    for a in range(5):
        total = None
        for b in range(5):
            term = D[b][a] * moved[b]
            total = term if total is None else total + term
        turned.append(jnp.where(inner, total, 0.0))
    turned[0] = turned[0] + jnp.where(after_first, pltpu.roll(turned[4], 1, 0), 0.0)
    for i in range(4):
        force[8 * i : 8 * i + 8, :] += turned[i]
    def slopes_of(plane):
        return [stencil(plane, coef_ref, base, stride) for base, stride, _, _ in axes]

    def last_layer(planes_ref, flux_ref, plane, slopes=None):
        edge = [planes_ref[2 * i : 2 * i + 2, :] for i in range(4)] + [plane]
        mm, me, em, ee = (flux_ref[4 + q : 5 + q, :] for q in range(4))
        edge_flux = [flux_ref[i : i + 1, :] for i in range(4)] + [(mm + me) + (em + ee)]
        grads = []
        for a in range(5):
            total = None
            for b in range(5):
                term = D[a][b] * edge[b]
                total = term if total is None else total + term
            grads.append(total)
        moved = [edge_flux[a] * grads[a] for a in range(5)]
        across = []
        for (gm, ge), am, ae in zip(slopes or slopes_of(plane), (mm + me, mm + em), (em + ee, me + ee)):
            across.append((gm, ge, am * gm, ae * ge))
        return grads, moved, across

    def last_terms(planes_ref, flux_ref, plane, slopes=None):
        grads, moved, across = last_layer(planes_ref, flux_ref, plane, slopes)
        terms = [moved[a][0:1, :] * grads[a][1:2, :] for a in range(5)]
        for gm, ge, fm, fe in across:
            terms[4] = terms[4] + fm[0:1, :] * gm[1:2, :] + fe[0:1, :] * ge[1:2, :]
        return terms

    def last_force(planes_ref, flux_ref, plane):
        _, moved, across = last_layer(planes_ref, flux_ref, plane)
        turned = []
        for a in range(5):
            total = None
            for b in range(5):
                term = D[b][a] * moved[b]
                total = term if total is None else total + term
            turned.append(total)
        for (base, stride, _, _), (_, _, fm, fe) in zip(axes, across):
            turned[4] = turned[4] + spread(fm, fe, coef_ref, base, stride)
        return turned

    @pl.when(jnp.logical_not(final))
    def _():
        to_behind.wait_recv()
        terms = last_terms(stage_u, stage_a, ghost[...])
        for m in range(events + 1):
            lanes = slice(128 * m, 128 * m + 128)
            for i in range(4):
                part[m, 4 * i + 3 : 4 * i + 4, :] += terms[i][:, lanes]
            part[m, 20:21, :] = terms[4][:, lanes]

    lead = e == events - 1
    for m in range(1, events):
        to = event_at(m)
        pltpu.make_async_remote_copy(
            part.at[to["event"]], recv.at[e], part_send, part_recv, to, MESH
        ).start()
    short_part = pltpu.make_async_remote_copy(
        part.at[events], recv_short.at[e], short_send, short_recv, {"event": events - 1}, MESH
    )
    pl.when(jnp.logical_not(lead))(short_part.start)
    recv[e] = part[e]

    force_ahead = pltpu.make_async_remote_copy(
        stage_f, carried, halo_send.at[3], halo_recv.at[3], cut_at(1), MESH
    )
    force_back = pltpu.make_async_remote_copy(
        stage_r, returned, halo_send.at[4], halo_recv.at[4], cut_at(-1), MESH
    )

    @pl.when(jnp.logical_not(final))
    def _():
        turned = last_force(stage_u, stage_a, ghost[...])
        stage_f[...] = turned[4]
        force_ahead.start()
        for i in range(4):
            for f in range(2):
                at = 8 * i + 4 * f + 3
                force[at : at + 1, :] += turned[i][f : f + 1, :]

    for n in range(5, 9):
        loads[n].wait()

    def edges_of(n):
        return [
            pltpu.make_async_remote_copy(src, dst, edge_send.at[n, c], edge_recv.at[n, c], cut_at(m), MESH)
            for c, (src, dst, m) in enumerate(
                (
                    (total_ref.at[n], halo.at[n, 0], 1),
                    (total_ref.at[n], halo.at[n, 1], -1),
                    (total_ref.at[n, pl.ds(16, 8)], halo_far.at[n, 0], 2),
                    (total_ref.at[n, pl.ds(16, 8)], halo_far.at[n, 1], -2),
                )
            )
        ]

    def slot(n):
        return e if n == 0 else events

    def tiles_of(n):
        return [
            pltpu.make_async_remote_copy(
                total_ref.at[n, pl.ds(0, 16)], wrap_rows.at[slot(n)], tile_send.at[n, m], tile_recv, {**event_at(m), "cuts": 0}, MESH
            )
            for m in order + [0]
        ]

    def extras_of(n):
        return [
            pltpu.make_async_remote_copy(
                total_ref.at[n, pl.ds(16, 8)],
                wrap_extra.at[slot(n)],
                extra_send.at[n, m],
                extra_recv,
                {**event_at(m), "cuts": 0},
                MESH,
            )
            for m in order + [0]
        ]

    def gathered(source, semaphore, n):
        some = source.at[pl.ds(0, events - 1)]
        pltpu.make_async_copy(some, some, semaphore).wait()
        total = source[0]
        for m in range(1, events):
            total = total + source[m]
        total_ref[n] = total
        ahead, behind, far_ahead, far_behind = edges_of(n)
        pl.when(final)(lambda: [copy.start() for copy in tiles_of(n)] and None)
        pl.when(before_final)(lambda: [copy.start() for copy in extras_of(n)] and None)
        pl.when(jnp.logical_not(final))(ahead.start)
        pl.when(s < slices - 2)(far_ahead.start)

    def smoothed(n):
        ahead, behind, far_ahead, far_behind = edges_of(n)
        behind.wait_recv()
        far_behind.wait_recv()
        pl.when(jnp.logical_not(first))(ahead.wait_recv)
        pl.when(s > 1)(far_ahead.wait_recv)
        parts = [halo[n, 0], total_ref[n], halo[n, 1]]
        tall = jnp.concatenate(
            [x[0:16, :] for x in parts] + [halo_far[n, 0]] + [x[16:24, :] for x in parts] + [halo_far[n, 1]],
            axis=0,
        )
        return jnp.dot(
            band_ref[:, 0:88], tall, precision=lax.Precision.HIGH, preferred_element_type=f32
        )

    def back_edges(n):
        _, behind, _, far_behind = edges_of(n)
        behind.start()
        far_behind.start()

    gathered(recv, part_recv, 0)

    @pl.when(lead)
    def _():
        recv_short[e] = part[events]
        gathered(recv_short, short_recv, 1)

    pl.when(first)(lambda: pl.semaphore_wait(ready, 2))
    pl.when(second)(lambda: pl.semaphore_wait(ready, 1))
    back_edges(0)
    pl.when(lead)(lambda: back_edges(1))

    cols[e] = smoothed(0)
    pairs = [
        pltpu.make_async_remote_copy(
            cols.at[pl.ds(events - 1, 2)],
            cols.at[pl.ds(events - 1, 2)],
            lone_send.at[m],
            cols_recv,
            {"event": m},
            MESH,
        )
        for m in range(events - 1)
    ]

    @pl.when(lead)
    def _():
        cols[events] = smoothed(1)
        for copy in pairs:
            copy.start()

    @pl.when(jnp.logical_not(lead))
    def _():
        for m in range(1, events):
            pltpu.make_async_remote_copy(
                cols.at[e], cols.at[e], cols_send, cols_recv, event_at(m), MESH
            ).start()

    @pl.when(first)
    def _():
        plane = stage_g[...]
        slopes = slopes_of(plane)
        planes_ahead.wait_recv()
        flux_ahead.wait_recv()
        terms = last_terms(tail_u, tail_a, plane, slopes)
        for i in range(5):
            wrap_terms[e, i : i + 1, :] = terms[i]
        for m in range(1, events):
            pltpu.make_async_remote_copy(
                wrap_terms.at[e], wrap_terms.at[e], terms_send, terms_recv, event_at(m), MESH
            ).start()

    @pl.when(first)
    def _():
        turned = last_force(tail_u, tail_a, stage_g[...])
        for i in range(4):
            stage_r[2 * i : 2 * i + 2, :] = turned[i]
        force_back.start()
        for f in range(2):
            force[4 * f : 4 * f + 1, :] += turned[4][f : f + 1, :]

    @pl.when(jnp.logical_not(first))
    def _():
        force_ahead.wait_recv()
        for f in range(2):
            force[4 * f : 4 * f + 1, :] += carried[f : f + 1, :]

    @pl.when(final)
    def _():
        force_back.wait_recv()
        for i in range(4):
            for f in range(2):
                at = 8 * i + 4 * f + 3
                force[at : at + 1, :] += returned[2 * i + f : 2 * i + f + 1, :]

    ends = planes_to_flat(
        [force[8 * i : 8 * i + 8, :] for i in range(4)], (rows_a, rows_b), lane1, row1
    )
    for f, (sign, now_out, speed_out) in enumerate(
        ((time_step, fdn_ref, fvn_ref), (-time_step, adn_ref, avn_ref))
    ):
        rows = (rows_a, rows_b)[f]
        for g in range(18):
            at, size = 1024 * g, 1024 if g < 17 else 16
            push = rows[8 * g : 8 * g + 8, :].reshape(1, 1024) if g < 17 else ends[f]
            mass = run_of(mass_flat, at, size).reshape(1, size)
            speed = flats[2 + f, 0:1, at : at + size] + (sign * mass) * push
            speed_out[0:1, at : at + size] = speed
            now_out[0:1, at : at + size] = flats[f, 0:1, at : at + size] - sign * speed
    nears = [
        pltpu.make_async_remote_copy(wrap_total, wrap_near, near_send.at[n], near_recv, cut_at(m), MESH)
        for n, m in enumerate((1, -1, -2))
    ]
    table = band_ref[...]

    def add(weights, rows):
        wrap_sum[...] += jnp.dot(
            weights, rows, precision=lax.Precision.HIGH, preferred_element_type=f32
        )

    def wide(ref, start, size):
        return jnp.concatenate([ref[m, start : start + size, :] for m in range(events + 1)], axis=1)

    @pl.when(first)
    def _():
        seven = wrap_terms.at[pl.ds(0, events - 1)]
        pltpu.make_async_copy(seven, seven, terms_recv).wait()
        total = wrap_terms[0]
        for m in range(1, events):
            total = total + wrap_terms[m]
        wrap_total[...] = total
        for copy in nears:
            copy.start()
        pltpu.make_async_copy(wrap_rows, wrap_rows, tile_recv).wait()
        pltpu.make_async_copy(wrap_extra, wrap_extra, extra_recv).wait()
        add(table[:, 88:93], total)
        weights = jnp.concatenate([table[:, 0:16], table[:, 48:56]], axis=1)
        add(weights, jnp.concatenate([wide(wrap_rows, 0, 16), wide(wrap_extra, 0, 8)], axis=0))

    for n, place in enumerate((second, final, before_final)):
        @pl.when(place)
        def _():
            nears[0].wait_recv()
            add(table[:, 93 + 5 * n : 98 + 5 * n], wrap_near[...])

    def got(count, semaphore):
        some = cols.at[pl.ds(0, count)]
        pltpu.make_async_copy(some, some, semaphore).wait()

    pl.when(lead)(lambda: got(events - 1, cols_recv))
    pl.when(jnp.logical_not(lead))(lambda: got(events, cols_recv))
    total = jnp.concatenate([cols[m] for m in range(events + 1)], axis=1) + wrap_sum[...]
    across = None
    for d in range(-cross_reach, cross_reach + 1):
        term = coef_ref[20 + d : 21 + d, :] * shifted(total, PZ * d)
        across = term if across is None else across + term
    total, across = across, None
    for d in range(-cross_reach, cross_reach + 1):
        term = coef_ref[29 + d : 30 + d, :] * shifted(total, d)
        across = term if across is None else across + term
    sk_ref[...] = across[:, 0:PYZ]
    pl.when(jnp.logical_not(lead))(lambda: got(events - 1, cols_send))
    seven = recv.at[pl.ds(0, events - 1)]
    pltpu.make_async_copy(seven, seven, part_send).wait()

    def sent(n):
        ahead, behind, far_ahead, far_behind = edges_of(n)
        behind.wait_send()
        far_behind.wait_send()
        pl.when(jnp.logical_not(final))(ahead.wait_send)
        pl.when(s < slices - 2)(far_ahead.wait_send)
        pl.when(final)(lambda: [copy.wait_send() for copy in tiles_of(n)] and None)
        pl.when(before_final)(lambda: [copy.wait_send() for copy in extras_of(n)] and None)

    sent(0)

    @pl.when(lead)
    def _():
        sent(1)
        for copy in pairs:
            copy.wait_send()

    @pl.when(first)
    def _():
        seven = wrap_terms.at[pl.ds(0, events - 1)]
        pltpu.make_async_copy(seven, seven, terms_send).wait()
        for copy in nears:
            copy.wait_send()

    pl.when(jnp.logical_not(lead))(short_part.wait_send)
    pl.when(jnp.logical_not(first))(to_behind.wait_send)
    pl.when(jnp.logical_not(final))(force_ahead.wait_send)
    pl.when(first)(force_back.wait_send)

    @pl.when(final)
    def _():
        planes_ahead.wait_send()
        flux_ahead.wait_send()


def store_kernel(a, b, c, d, k, a_hbm, b_hbm, c_hbm, d_hbm, k_hbm, sem):
    pairs = ((k, k_hbm), (a, a_hbm), (b, b_hbm), (c, c_hbm), (d, d_hbm))
    copies = [pltpu.make_async_copy(src, dst, sem.at[n]) for n, (src, dst) in enumerate(pairs)]
    for copy in copies:
        copy.start()
    for copy in copies:
        copy.wait()


def on_device(events, slices):
    def run(fd, fv, ad, av, inverse_mass, shear, connectivity, face_points, count):
        vmem = pl.BlockSpec(memory_space=pltpu.VMEM)
        there = pl.BlockSpec(memory_space=pltpu.HBM)
        stay = lambda x: pltpu.with_memory_space_constraint(x, pltpu.HBM)
        f32 = jnp.float32
        flat = jax.ShapeDtypeStruct((1, NPTS), f32)
        table = jax.ShapeDtypeStruct((PXU, PYZ), f32)
        big = lambda *dims: pltpu.VMEM((*dims, LANES), f32)
        small = lambda *dims: pltpu.VMEM((*dims, 128), f32)
        dma = pltpu.SemaphoreType.DMA
        outs = pl.pallas_call(
            functools.partial(step_kernel, events, slices),
            out_shape=(flat, flat, flat, flat, table),
            in_specs=[there] * 7 + [pl.BlockSpec(memory_space=pltpu.SMEM)] + [there] * 2,
            out_specs=(vmem,) * 5,
            scratch_shapes=[
                pltpu.VMEM((4, 1, NPTS), f32),
                pltpu.VMEM((NPTS,), f32),
                small(280),
                small(8),
                small(136),
                small(136),
                pltpu.VMEM((125, 256), f32),
                pltpu.VMEM((8, 256), jnp.int32),
                big(56),
                small(16),
                big(32),
                pltpu.VMEM((2, 624, 256), jnp.bfloat16),
                big(624),
                big(40),
                big(32),
                big(32),
                big(32),
                big(32),
                big(2),
                big(8),
                big(2),
                big(8),
                big(8),
                big(2),
                big(2),
                big(8),
                big(8),
                big(8),
                big(32),
                big(32),
                small(events + 1, 24),
                small(events, 24),
                small(events, 24),
                small(2, 24),
                small(2, 2, 24),
                small(2, 2, 8),
                small(events + 1, 16),
                small(events + 1, 16),
                small(events + 1, 8),
                big(events, 5),
                big(5),
                big(5),
                big(16),
                dma((9,)),
                dma((5,)),
                dma((5,)),
                dma,
                dma,
                dma,
                dma,
                dma((2, 4)),
                dma((2, 4)),
                dma,
                dma,
                dma((events - 1,)),
                pltpu.SemaphoreType.REGULAR,
                dma((2, events)),
                dma,
                dma((2, events)),
                dma,
                dma,
                dma,
                dma((3,)),
                dma,
            ],
            compiler_params=pltpu.CompilerParams(
                collective_id=0, has_side_effects=True, vmem_limit_bytes=40 << 20
            ),
        )(
            *map(stay, (fd, fv, ad, av, inverse_mass, shear, connectivity)),
            count,
            stay(jnp.asarray(lane_tables())),
            stay(jnp.asarray(band_table())),
        )
        fdn, fvn, adn, avn, sk = pl.pallas_call(
            store_kernel,
            out_shape=(flat, flat, flat, flat, table),
            in_specs=[vmem] * 5,
            out_specs=(there,) * 5,
            scratch_shapes=[dma((5,))],
            compiler_params=pltpu.CompilerParams(vmem_limit_bytes=4 << 20),
        )(*outs)
        return fdn, fvn, adn, avn, sk

    return run


def solution(mesh):
    both = P("event", "cuts")
    return jax.shard_map(
        on_device(mesh.shape["event"], mesh.shape["cuts"]),
        mesh=mesh,
        in_specs=(
            both,
            both,
            both,
            both,
            P("cuts"),
            P(None, "cuts"),
            P(None, "cuts"),
            P("cuts", None),
            P("cuts"),
        ),
        out_specs=(both, both, both, both, P("cuts", None)),
        check_vma=False,
    )
```

```python
import functools

import jax
import jax.numpy as jnp
import numpy as np
from jax import lax
from jax.experimental import pallas as pl
from jax.experimental.pallas import tpu as pltpu
from jax.sharding import PartitionSpec as P

NGLL = 5
PXU = 16
PY = 33
PZ = 33
PYZ = 1089
NPTS = 17424
LANES = 1152

time_step = 0.02
cross_sigma = 1.5
cross_reach = 4

MESH = pl.DeviceIdType.MESH


def gll_tables():
    nodes = np.array([-1.0, -np.sqrt(3.0 / 7.0), 0.0, np.sqrt(3.0 / 7.0), 1.0])
    quad = np.array([0.1, 49.0 / 90.0, 32.0 / 45.0, 49.0 / 90.0, 0.1])
    bary = np.array(
        [1.0 / np.prod([nodes[a] - nodes[b] for b in range(5) if b != a]) for a in range(5)]
    )
    deriv = np.zeros((5, 5))
    for a in range(5):
        for b in range(5):
            if b != a:
                deriv[a, b] = bary[b] / bary[a] / (nodes[a] - nodes[b])
        deriv[a, a] = -np.sum(deriv[a])
    cube = (quad[:, None, None] * quad[None, :, None] * quad[None, None, :]).reshape(125)
    return deriv.astype(np.float32), cube.astype(np.float32)


DERIV, CUBE = gll_tables()
D = [[float(DERIV[a, b]) for b in range(5)] for a in range(5)]


def lane_tables():
    lane = np.arange(LANES)
    live = lane < PYZ
    y, z = lane // PZ, lane % PZ
    rows = []
    for pos, extent in ((y, PY), (z, PZ)):
        for d in range(-3, 5):
            node = pos % 4
            inside = live & (pos < extent - 1) & (node + d >= 0) & (node + d <= 4)
            value = DERIV[node, np.clip(node + d, 0, 4)]
            rows.append(np.where(inside, value, 0.0))
    for pos, extent in ((y, PY), (z, PZ)):
        weight = lambda d: np.exp(-d * d / (2.0 * cross_sigma * cross_sigma))
        norm = np.zeros(LANES)
        for d in range(-cross_reach, cross_reach + 1):
            norm += np.where((pos + d >= 0) & (pos + d < extent), weight(d), 0.0)
        for d in range(-cross_reach, cross_reach + 1):
            inside = live & (pos + d >= 0) & (pos + d < extent)
            rows.append(np.where(inside, weight(d) / norm, 0.0))
    rows = np.stack(rows).astype(np.float32)
    return np.pad(rows, ((0, 56 - rows.shape[0]), (0, 0)))


def band_table():
    sigma = PXU / 4.0
    w = lambda d: np.exp(-d * d / (2.0 * sigma * sigma))
    norm = np.sum(w(np.arange(-PXU, PXU + 1).astype(np.float64)))

    def table(places):
        gap = places[None, :] - np.arange(PXU)[:, None]
        return np.where(np.abs(gap) <= PXU, w(gap.astype(np.float64)) / norm, 0.0)

    rows = table(np.arange(-PXU, 2 * PXU)).reshape(PXU, 3, 4, 4).transpose(0, 1, 3, 2).reshape(PXU, 48)
    places = PXU * np.arange(-2, 3)[:, None] + np.array([-4, -3, -2, -1, 16])[None, :]
    extra = np.pad(table(places.reshape(25)).reshape(PXU, 5, 5), ((0, 0), (0, 0), (0, 3)))
    wrapped = table((np.array([-4, -20, 12, 28])[:, None] + np.arange(5)[None, :]).reshape(20))
    both = np.concatenate([rows, extra.reshape(PXU, 40), wrapped], axis=1)
    return np.pad(-both, ((0, 0), (0, 20))).astype(np.float32)


def shifted(x, step):
    shift = (-step) % LANES
    return x if shift == 0 else pltpu.roll(x, shift, 1)


def stencil(u, coef_ref, base, stride):
    main = end = None
    for d in range(-4, 5):
        moved = shifted(u, stride * d)
        if d >= -3:
            row = base + d + 3
            term = coef_ref[row : row + 1, :] * moved
            main = term if main is None else main + term
        if d <= 0:
            term = D[4][4 + d] * moved
            end = term if end is None else end + term
    return main, end


def spread(fm, fe, coef_ref, base, stride):
    total = None
    for d in range(-4, 5):
        term = None
        if d >= -3:
            row = base + d + 3
            term = coef_ref[row : row + 1, :] * fm
        if d <= 0:
            part = D[4][4 + d] * fe
            term = part if term is None else term + part
        term = shifted(term, -stride * d)
        total = term if total is None else total + term
    return total


FIRST = [PYZ * i // 128 for i in range(4)]
LEAD = [PYZ * i % 128 for i in range(4)]
GROUP = 34


def lane_starts(i, lane_row):
    return LEAD[i] + 4 * (lane_row % 4)


def run_of(flat_ref, start, size):
    if len(flat_ref.shape) == 1:
        return flat_ref[start : start + size]
    return flat_ref[0:1, start : start + size]


def flat_to_rows(flat_ref, both, first):
    for g in range(17):
        both[first + 8 * g : first + 8 * g + 8, :] = run_of(flat_ref, 1024 * g, 1024).reshape(8, 128)


def planes(both, tail_row, i, lane, row):
    tiles = []
    for t in range(10):
        at = FIRST[i] + t
        tile = both[pl.ds(at, 8, stride=GROUP), :]
        if i == 3 and t == 9:
            tile = jnp.where(row == 3, tail_row, tile)
        if LEAD[i]:
            tile = pltpu.roll(tile, 128 - LEAD[i], 1)
        tile = jnp.where(row % 2 == 1, pltpu.roll(tile, 124, 1), tile)
        tiles.append(jnp.where(row % 4 >= 2, pltpu.roll(tile, 120, 1), tile))
    keep = lane < 128 - lane_starts(i, row)
    return jnp.concatenate([jnp.where(keep, tiles[t], tiles[t + 1]) for t in range(9)], axis=1)


def planes_to_flat(slabs, rows_refs, lane, row):
    before = None
    done = []
    for i in range(4):
        tiles = []
        for t in range(9):
            tile = slabs[i][:, 128 * t : 128 * t + 128]
            if LEAD[i]:
                tile = pltpu.roll(tile, LEAD[i], 1)
            tile = jnp.where(row % 2 == 1, pltpu.roll(tile, 4, 1), tile)
            tiles.append(jnp.where(row % 4 >= 2, pltpu.roll(tile, 8, 1), tile))
        start = lane < lane_starts(i, row)
        count = (FIRST + [GROUP])[i + 1] - FIRST[i]
        for t in range(count):
            low = tiles[t - 1] if t else before
            done.append(tiles[t] if low is None else jnp.where(start, low, tiles[t]))
        before = tiles[8] if count == 9 else jnp.where(start, tiles[7], tiles[8])
    done[0] = jnp.where(lane < lane_starts(0, row), pltpu.roll(before, 1, 0), done[0])
    for f in range(2):
        rows = rows_refs[f]
        for g in range(GROUP):
            rows[pl.ds(g, 4, stride=GROUP), :] = done[g][4 * f : 4 * f + 4, :]
    return [before[4 * f + 3 : 4 * f + 4, 0:16] for f in range(2)]


def step_kernel(
    events,
    slices,
    fd_hbm,
    fv_hbm,
    ad_hbm,
    av_hbm,
    mass_hbm,
    shear_hbm,
    conn_hbm,
    count_ref,
    coef_hbm,
    band_hbm,
    fdn_ref,
    fvn_ref,
    adn_ref,
    avn_ref,
    sk_ref,
    flats,
    mass_flat,
    both,
    tails,
    rows_a,
    rows_b,
    shear_ref,
    conn_ref,
    coef_ref,
    band_ref,
    u_ref,
    lhs,
    placed,
    ax,
    aym,
    aye,
    azm,
    aze,
    carried,
    returned,
    ghost,
    tail_u,
    tail_a,
    stage_g,
    stage_f,
    stage_r,
    stage_u,
    stage_a,
    force,
    kern,
    part,
    recv,
    recv_short,
    total_ref,
    halo,
    halo_far,
    cols,
    wrap_rows,
    wrap_extra,
    wrap_terms,
    wrap_total,
    wrap_near,
    wrap_sum,
    load_sem,
    halo_send,
    halo_recv,
    part_send,
    part_recv,
    short_send,
    short_recv,
    edge_send,
    edge_recv,
    cols_send,
    cols_recv,
    lone_send,
    ready,
    tile_send,
    tile_recv,
    extra_send,
    extra_recv,
    terms_send,
    terms_recv,
    near_send,
    near_recv,
):
    f32 = jnp.float32
    e = lax.axis_index("event")
    s = lax.axis_index("cuts")
    first, final = s == 0, s == slices - 1
    second, before_final = s == 1, s == slices - 2
    cut_at = lambda m: {"cuts": lax.rem(s + m + slices, slices)}

    barrier = pltpu.get_barrier_semaphore()

    def greet_cut(m):
        pl.semaphore_signal(barrier, inc=1, device_id=cut_at(m), device_id_type=MESH)

    greet_cut(-1)
    greet_cut(-2)
    pl.when(jnp.logical_not(final))(lambda: greet_cut(1))
    pl.when(s < slices - 2)(lambda: greet_cut(2))

    def event_at(m):
        return {"event": lax.rem(e + m, events)}

    order = sorted(range(1, events), key=lambda m: abs(m - events // 2))
    for m in order:
        pl.semaphore_signal(barrier, inc=1, device_id=event_at(m), device_id_type=MESH)

    def greet(cut):
        for m in range(1, events):
            to = {**event_at(m), "cuts": cut}
            pl.semaphore_signal(barrier, inc=1, device_id=to, device_id_type=MESH)

    @pl.when(first)
    def _():
        greet(slices - 1)
        greet(slices - 2)


    @pl.when(first)
    def _():
        for n in range(2):
            halo[n, 0] = jnp.zeros((24, 128), jnp.float32)

    @pl.when(s <= 1)
    def _():
        for n in range(2):
            halo_far[n, 0] = jnp.zeros((8, 128), jnp.float32)

    wrap_sum[...] = jnp.zeros((PXU, LANES), jnp.float32)

    loads = [
        pltpu.make_async_copy(src, dst, load_sem.at[n])
        for n, (src, dst) in enumerate(
            (
                (conn_hbm.at[pl.ds(0, 8), :], conn_ref),
                (shear_hbm, shear_ref),
                (fd_hbm, flats.at[0]),
                (ad_hbm, flats.at[1]),
                (coef_hbm, coef_ref),
                (fv_hbm, flats.at[2]),
                (av_hbm, flats.at[3]),
                (mass_hbm, mass_flat),
                (band_hbm, band_ref),
            )
        )
    ]
    for load in loads:
        load.start()

    row = lax.broadcasted_iota(jnp.int32, (8, LANES), 0)
    row1 = lax.broadcasted_iota(jnp.int32, (8, 128), 0)
    lane1 = lax.broadcasted_iota(jnp.int32, (8, 128), 1)

    def slabs_of(first, second):
        flat_to_rows(first, both, 0)
        flat_to_rows(second, both, 136)
        tails[...] = jnp.zeros((8, 128), f32)
        tails[0:1, 0:16] = run_of(first, 17408, 16).reshape(1, 16)
        both[272:280, :] = jnp.zeros((8, 128), f32)
        both[272:273, 0:16] = run_of(second, 17408, 16).reshape(1, 16)
        return [planes(both, tails[0:1, :], i, lane1, row1) for i in range(4)]

    for n in (0, 1):
        loads[n].wait()
    corner = conn_ref[0:1, :]
    layer = sum(jnp.where(corner >= 4 * PYZ * n, 1, 0) for n in (1, 2, 3))
    base = jnp.broadcast_to(corner - 4 * PYZ * layer, (128, 256)).T
    wide_row = lax.broadcasted_iota(jnp.int32, (8, 256), 0)
    slot = lax.broadcasted_iota(jnp.int32, (8, 256), 1)
    own = jnp.where((wide_row % 4 == layer) & (slot < count_ref[0]), 1.0, 0.0)

    def flux_rows(c, jk):
        if jk == 25:
            return jnp.zeros((8, 256), f32)
        near = 50 * c + jk
        value = float(CUBE[near]) * shear_ref[near : near + 1, :]
        if c < 2:
            far = near + 25
            value = jnp.where(wide_row < 4, value, float(CUBE[far]) * shear_ref[far : far + 1, :])
        else:
            value = jnp.where(wide_row < 4, value, 0.0)
        return value * own

    for c in range(3):
        for pair in range(13):
            value = jnp.concatenate([flux_rows(c, 2 * pair), flux_rows(c, 2 * pair + 1)], axis=0)
            at = 208 * c + 16 * pair
            hi = value.astype(jnp.bfloat16)
            lhs[0, at : at + 16, :] = hi
            lhs[1, at : at + 16, :] = (value - hi.astype(f32)).astype(jnp.bfloat16)
    lane_wide = lax.broadcasted_iota(jnp.int32, (256, 128), 1)
    pick = jnp.concatenate(
        [jnp.where(base == lane_wide + 128 * t, 1.0, 0.0).astype(jnp.bfloat16) for t in range(9)], axis=1
    )
    placed[...] = jnp.dot(lhs[0], pick, preferred_element_type=f32) + jnp.dot(
        lhs[1], pick, preferred_element_type=f32
    )

    loads[2].wait()
    loads[3].wait()
    for i, value in enumerate(slabs_of(flats.at[0], flats.at[1])):
        u_ref[8 * i : 8 * i + 8, :] = value
    for f in range(2):
        stage_g[f : f + 1, :] = u_ref[4 * f : 4 * f + 1, :]
        for i in range(4):
            at = 8 * i + 4 * f + 3
            stage_u[2 * i + f : 2 * i + f + 1, :] = u_ref[at : at + 1, :]

    more = (events - 1) * jnp.where(s >= slices - 2, 1, 0)
    fewer = 2 * jnp.where(first, 1, 0) + jnp.where(second, 1, 0)
    pl.semaphore_wait(barrier, events + 3 + more - fewer)

    def tell(m):
        pl.semaphore_signal(ready, inc=1, device_id=cut_at(m), device_id_type=MESH)

    pl.when(final)(lambda: tell(1))
    pl.when(s >= slices - 2)(lambda: tell(2))
    to_behind = pltpu.make_async_remote_copy(
        stage_g, ghost, halo_send.at[0], halo_recv.at[0], cut_at(-1), MESH
    )
    planes_ahead = pltpu.make_async_remote_copy(
        stage_u, tail_u, halo_send.at[1], halo_recv.at[1], cut_at(1), MESH
    )
    pl.when(jnp.logical_not(first))(to_behind.start)
    pl.when(final)(planes_ahead.start)

    twice = lambda x: jnp.concatenate([x, x], axis=0)
    kinds = (aym, aye, azm, aze)
    for c in (2, 0, 1):
        sums = [None] * 4
        for j in range(5):
            for k in range(5):
                at = 208 * c + 8 * (5 * j + k)
                moved = shifted(placed[at : at + 8, :], -(PZ * j + k))
                q = 2 * (j == 4) + (k == 4)
                sums[q] = moved if sums[q] is None else sums[q] + moved
        mm, me, em, ee = sums
        whole = (mm + me) + (em + ee)
        pairs = (mm + me, em + ee, mm + em, me + ee)
        if c == 2:
            ax[32:40, :] = twice(whole[0:4, :])
            for q in range(4):
                stage_a[4 + q : 5 + q, :] = sums[q][3:4, :]
                moved = pltpu.roll(twice(pairs[q][0:4, :]), 1, 0)
                kinds[q][0:8, :] = jnp.where(row % 4 == 0, 0.0, moved)
        else:
            for half in range(2):
                i = 2 * c + half
                some = slice(4 * half, 4 * half + 4)
                ax[8 * i : 8 * i + 8, :] = twice(whole[some, :])
                stage_a[i : i + 1, :] = whole[4 * half + 3 : 4 * half + 4, :]
                for q in range(4):
                    value = twice(pairs[q][some, :])
                    if i == 0:
                        value = value + kinds[q][0:8, :]
                    kinds[q][8 * i : 8 * i + 8, :] = value

    flux_ahead = pltpu.make_async_remote_copy(
        stage_a, tail_a, halo_send.at[2], halo_recv.at[2], cut_at(1), MESH
    )
    pl.when(final)(flux_ahead.start)

    loads[4].wait()
    axes = ((0, PZ, aym, aye), (8, 1, azm, aze))
    for i in range(4):
        at = 8 * i
        u = u_ref[at : at + 8, :]
        ksum = tsum = None
        for base, stride, m_ref, e_ref in axes:
            gm, ge = stencil(u, coef_ref, base, stride)
            fm, fe = m_ref[at : at + 8, :] * gm, e_ref[at : at + 8, :] * ge
            term = fm * pltpu.roll(gm, 4, 0) + fe * pltpu.roll(ge, 4, 0)
            ksum = term if ksum is None else ksum + term
            term = spread(fm, fe, coef_ref, base, stride)
            tsum = term if tsum is None else tsum + term
        kern[at : at + 8, :] = ksum
        force[at : at + 8, :] = tsum

    slab = [u_ref[8 * i : 8 * i + 8, :] for i in range(4)]
    slab.append(pltpu.roll(slab[0], 7, 0))
    grads = []
    for a in range(5):
        total = None
        for b in range(5):
            term = D[a][b] * slab[b]
            total = term if total is None else total + term
        grads.append(total)
    moved = [ax[8 * a : 8 * a + 8, :] * grads[a] for a in range(5)]
    prods = [moved[a] * pltpu.roll(grads[a], 4, 0) for a in range(5)]
    inner = row % 4 < 3
    after_first = row % 4 > 0
    terms = [kern[8 * i : 8 * i + 8, :] + jnp.where(inner, prods[i], 0.0) for i in range(4)]
    terms[0] = terms[0] + jnp.where(after_first, pltpu.roll(prods[4], 1, 0), 0.0)
    for half in range(2):
        nodes = jnp.where(row < 4, terms[2 * half], terms[2 * half + 1])
        for m in range(events + 1):
            part[m, 8 * half : 8 * half + 8, :] = nodes[:, 128 * m : 128 * m + 128]
    for m in range(events + 1):
        part[m, 16:24, :] = jnp.zeros((8, 128), f32)
    turned = []
    for a in range(5):
        total = None
        for b in range(5):
            term = D[b][a] * moved[b]
            total = term if total is None else total + term
        turned.append(jnp.where(inner, total, 0.0))
    turned[0] = turned[0] + jnp.where(after_first, pltpu.roll(turned[4], 1, 0), 0.0)
    for i in range(4):
        force[8 * i : 8 * i + 8, :] += turned[i]
    def slopes_of(plane):
        return [stencil(plane, coef_ref, base, stride) for base, stride, _, _ in axes]

    def last_layer(planes_ref, flux_ref, plane, slopes=None):
        edge = [planes_ref[2 * i : 2 * i + 2, :] for i in range(4)] + [plane]
        mm, me, em, ee = (flux_ref[4 + q : 5 + q, :] for q in range(4))
        edge_flux = [flux_ref[i : i + 1, :] for i in range(4)] + [(mm + me) + (em + ee)]
        grads = []
        for a in range(5):
            total = None
            for b in range(5):
                term = D[a][b] * edge[b]
                total = term if total is None else total + term
            grads.append(total)
        moved = [edge_flux[a] * grads[a] for a in range(5)]
        across = []
        for (gm, ge), am, ae in zip(slopes or slopes_of(plane), (mm + me, mm + em), (em + ee, me + ee)):
            across.append((gm, ge, am * gm, ae * ge))
        return grads, moved, across

    def last_terms(planes_ref, flux_ref, plane, slopes=None):
        grads, moved, across = last_layer(planes_ref, flux_ref, plane, slopes)
        terms = [moved[a][0:1, :] * grads[a][1:2, :] for a in range(5)]
        for gm, ge, fm, fe in across:
            terms[4] = terms[4] + fm[0:1, :] * gm[1:2, :] + fe[0:1, :] * ge[1:2, :]
        return terms

    def last_force(planes_ref, flux_ref, plane):
        _, moved, across = last_layer(planes_ref, flux_ref, plane)
        turned = []
        for a in range(5):
            total = None
            for b in range(5):
                term = D[b][a] * moved[b]
                total = term if total is None else total + term
            turned.append(total)
        for (base, stride, _, _), (_, _, fm, fe) in zip(axes, across):
            turned[4] = turned[4] + spread(fm, fe, coef_ref, base, stride)
        return turned

    @pl.when(jnp.logical_not(final))
    def _():
        to_behind.wait_recv()
        terms = last_terms(stage_u, stage_a, ghost[...])
        for m in range(events + 1):
            lanes = slice(128 * m, 128 * m + 128)
            for i in range(4):
                part[m, 4 * i + 3 : 4 * i + 4, :] += terms[i][:, lanes]
            part[m, 20:21, :] = terms[4][:, lanes]

    lead = e == events - 1
    for m in order:
        to = event_at(m)
        pltpu.make_async_remote_copy(
            part.at[to["event"]], recv.at[e], part_send, part_recv, to, MESH
        ).start()
    short_part = pltpu.make_async_remote_copy(
        part.at[events], recv_short.at[e], short_send, short_recv, {"event": events - 1}, MESH
    )
    pl.when(jnp.logical_not(lead))(short_part.start)
    recv[e] = part[e]

    force_ahead = pltpu.make_async_remote_copy(
        stage_f, carried, halo_send.at[3], halo_recv.at[3], cut_at(1), MESH
    )
    force_back = pltpu.make_async_remote_copy(
        stage_r, returned, halo_send.at[4], halo_recv.at[4], cut_at(-1), MESH
    )

    @pl.when(jnp.logical_not(final))
    def _():
        turned = last_force(stage_u, stage_a, ghost[...])
        stage_f[...] = turned[4]
        force_ahead.start()
        for i in range(4):
            for f in range(2):
                at = 8 * i + 4 * f + 3
                force[at : at + 1, :] += turned[i][f : f + 1, :]

    for n in range(5, 9):
        loads[n].wait()

    def edges_of(n):
        return [
            pltpu.make_async_remote_copy(src, dst, edge_send.at[n, c], edge_recv.at[n, c], cut_at(m), MESH)
            for c, (src, dst, m) in enumerate(
                (
                    (total_ref.at[n], halo.at[n, 0], 1),
                    (total_ref.at[n], halo.at[n, 1], -1),
                    (total_ref.at[n, pl.ds(16, 8)], halo_far.at[n, 0], 2),
                    (total_ref.at[n, pl.ds(16, 8)], halo_far.at[n, 1], -2),
                )
            )
        ]

    def slot(n):
        return e if n == 0 else events

    def tiles_of(n):
        return [
            pltpu.make_async_remote_copy(
                total_ref.at[n, pl.ds(0, 16)], wrap_rows.at[slot(n)], tile_send.at[n, m], tile_recv, {**event_at(m), "cuts": 0}, MESH
            )
            for m in order + [0]
        ]

    def extras_of(n):
        return [
            pltpu.make_async_remote_copy(
                total_ref.at[n, pl.ds(16, 8)],
                wrap_extra.at[slot(n)],
                extra_send.at[n, m],
                extra_recv,
                {**event_at(m), "cuts": 0},
                MESH,
            )
            for m in order + [0]
        ]

    def gathered(source, semaphore, n):
        some = source.at[pl.ds(0, events - 1)]
        pltpu.make_async_copy(some, some, semaphore).wait()
        total = source[0]
        for m in range(1, events):
            total = total + source[m]
        total_ref[n] = total
        ahead, behind, far_ahead, far_behind = edges_of(n)
        pl.when(final)(lambda: [copy.start() for copy in tiles_of(n)] and None)
        pl.when(before_final)(lambda: [copy.start() for copy in extras_of(n)] and None)
        pl.when(jnp.logical_not(final))(ahead.start)
        pl.when(s < slices - 2)(far_ahead.start)

    def smoothed(n):
        ahead, behind, far_ahead, far_behind = edges_of(n)
        behind.wait_recv()
        far_behind.wait_recv()
        pl.when(jnp.logical_not(first))(ahead.wait_recv)
        pl.when(s > 1)(far_ahead.wait_recv)
        parts = [halo[n, 0], total_ref[n], halo[n, 1]]
        tall = jnp.concatenate(
            [x[0:16, :] for x in parts] + [halo_far[n, 0]] + [x[16:24, :] for x in parts] + [halo_far[n, 1]],
            axis=0,
        )
        return jnp.dot(
            band_ref[:, 0:88], tall, precision=lax.Precision.HIGH, preferred_element_type=f32
        )

    def back_edges(n):
        _, behind, _, far_behind = edges_of(n)
        behind.start()
        far_behind.start()

    gathered(recv, part_recv, 0)

    @pl.when(lead)
    def _():
        recv_short[e] = part[events]
        gathered(recv_short, short_recv, 1)

    pl.when(first)(lambda: pl.semaphore_wait(ready, 2))
    pl.when(second)(lambda: pl.semaphore_wait(ready, 1))
    back_edges(0)
    pl.when(lead)(lambda: back_edges(1))

    cols[e] = smoothed(0)
    pairs = [
        pltpu.make_async_remote_copy(
            cols.at[pl.ds(events - 1, 2)],
            cols.at[pl.ds(events - 1, 2)],
            lone_send.at[m],
            cols_recv,
            {"event": m},
            MESH,
        )
        for m in range(events - 1)
    ]

    @pl.when(lead)
    def _():
        cols[events] = smoothed(1)
        for copy in pairs:
            copy.start()

    @pl.when(jnp.logical_not(lead))
    def _():
        for m in order:
            pltpu.make_async_remote_copy(
                cols.at[e], cols.at[e], cols_send, cols_recv, event_at(m), MESH
            ).start()

    @pl.when(first)
    def _():
        plane = stage_g[...]
        slopes = slopes_of(plane)
        planes_ahead.wait_recv()
        flux_ahead.wait_recv()
        terms = last_terms(tail_u, tail_a, plane, slopes)
        for i in range(5):
            wrap_terms[e, i : i + 1, :] = terms[i]
        for m in order:
            pltpu.make_async_remote_copy(
                wrap_terms.at[e], wrap_terms.at[e], terms_send, terms_recv, event_at(m), MESH
            ).start()

    @pl.when(first)
    def _():
        turned = last_force(tail_u, tail_a, stage_g[...])
        for i in range(4):
            stage_r[2 * i : 2 * i + 2, :] = turned[i]
        force_back.start()
        for f in range(2):
            force[4 * f : 4 * f + 1, :] += turned[4][f : f + 1, :]

    @pl.when(jnp.logical_not(first))
    def _():
        force_ahead.wait_recv()
        for f in range(2):
            force[4 * f : 4 * f + 1, :] += carried[f : f + 1, :]

    @pl.when(final)
    def _():
        force_back.wait_recv()
        for i in range(4):
            for f in range(2):
                at = 8 * i + 4 * f + 3
                force[at : at + 1, :] += returned[2 * i + f : 2 * i + f + 1, :]

    ends = planes_to_flat(
        [force[8 * i : 8 * i + 8, :] for i in range(4)], (rows_a, rows_b), lane1, row1
    )
    for f, (sign, now_out, speed_out) in enumerate(
        ((time_step, fdn_ref, fvn_ref), (-time_step, adn_ref, avn_ref))
    ):
        rows = (rows_a, rows_b)[f]
        for g in range(18):
            at, size = 1024 * g, 1024 if g < 17 else 16
            push = rows[8 * g : 8 * g + 8, :].reshape(1, 1024) if g < 17 else ends[f]
            mass = run_of(mass_flat, at, size).reshape(1, size)
            speed = flats[2 + f, 0:1, at : at + size] + (sign * mass) * push
            speed_out[0:1, at : at + size] = speed
            now_out[0:1, at : at + size] = flats[f, 0:1, at : at + size] - sign * speed
    nears = [
        pltpu.make_async_remote_copy(wrap_total, wrap_near, near_send.at[n], near_recv, cut_at(m), MESH)
        for n, m in enumerate((1, -1, -2))
    ]
    table = band_ref[...]

    def add(weights, rows):
        wrap_sum[...] += jnp.dot(
            weights, rows, precision=lax.Precision.HIGH, preferred_element_type=f32
        )

    def wide(ref, start, size):
        return jnp.concatenate([ref[m, start : start + size, :] for m in range(events + 1)], axis=1)

    @pl.when(first)
    def _():
        seven = wrap_terms.at[pl.ds(0, events - 1)]
        pltpu.make_async_copy(seven, seven, terms_recv).wait()
        total = wrap_terms[0]
        for m in range(1, events):
            total = total + wrap_terms[m]
        wrap_total[...] = total
        for copy in nears:
            copy.start()
        pltpu.make_async_copy(wrap_rows, wrap_rows, tile_recv).wait()
        pltpu.make_async_copy(wrap_extra, wrap_extra, extra_recv).wait()
        add(table[:, 88:93], total)
        weights = jnp.concatenate([table[:, 0:16], table[:, 48:56]], axis=1)
        add(weights, jnp.concatenate([wide(wrap_rows, 0, 16), wide(wrap_extra, 0, 8)], axis=0))

    for n, place in enumerate((second, final, before_final)):
        @pl.when(place)
        def _():
            nears[0].wait_recv()
            add(table[:, 93 + 5 * n : 98 + 5 * n], wrap_near[...])

    def got(count, semaphore):
        some = cols.at[pl.ds(0, count)]
        pltpu.make_async_copy(some, some, semaphore).wait()

    pl.when(lead)(lambda: got(events - 1, cols_recv))
    pl.when(jnp.logical_not(lead))(lambda: got(events, cols_recv))
    total = jnp.concatenate([cols[m] for m in range(events + 1)], axis=1) + wrap_sum[...]
    across = None
    for d in range(-cross_reach, cross_reach + 1):
        term = coef_ref[20 + d : 21 + d, :] * shifted(total, PZ * d)
        across = term if across is None else across + term
    total, across = across, None
    for d in range(-cross_reach, cross_reach + 1):
        term = coef_ref[29 + d : 30 + d, :] * shifted(total, d)
        across = term if across is None else across + term
    sk_ref[...] = across[:, 0:PYZ]
    pl.when(jnp.logical_not(lead))(lambda: got(events - 1, cols_send))
    seven = recv.at[pl.ds(0, events - 1)]
    pltpu.make_async_copy(seven, seven, part_send).wait()

    def sent(n):
        ahead, behind, far_ahead, far_behind = edges_of(n)
        behind.wait_send()
        far_behind.wait_send()
        pl.when(jnp.logical_not(final))(ahead.wait_send)
        pl.when(s < slices - 2)(far_ahead.wait_send)
        pl.when(final)(lambda: [copy.wait_send() for copy in tiles_of(n)] and None)
        pl.when(before_final)(lambda: [copy.wait_send() for copy in extras_of(n)] and None)

    sent(0)

    @pl.when(lead)
    def _():
        sent(1)
        for copy in pairs:
            copy.wait_send()

    @pl.when(first)
    def _():
        seven = wrap_terms.at[pl.ds(0, events - 1)]
        pltpu.make_async_copy(seven, seven, terms_send).wait()
        for copy in nears:
            copy.wait_send()

    pl.when(jnp.logical_not(lead))(short_part.wait_send)
    pl.when(jnp.logical_not(first))(to_behind.wait_send)
    pl.when(jnp.logical_not(final))(force_ahead.wait_send)
    pl.when(first)(force_back.wait_send)

    @pl.when(final)
    def _():
        planes_ahead.wait_send()
        flux_ahead.wait_send()


def store_kernel(a, b, c, d, k, a_hbm, b_hbm, c_hbm, d_hbm, k_hbm, sem):
    pairs = ((k, k_hbm), (a, a_hbm), (b, b_hbm), (c, c_hbm), (d, d_hbm))
    copies = [pltpu.make_async_copy(src, dst, sem.at[n]) for n, (src, dst) in enumerate(pairs)]
    for copy in copies:
        copy.start()
    for copy in copies:
        copy.wait()


def on_device(events, slices):
    def run(fd, fv, ad, av, inverse_mass, shear, connectivity, face_points, count):
        vmem = pl.BlockSpec(memory_space=pltpu.VMEM)
        there = pl.BlockSpec(memory_space=pltpu.HBM)
        stay = lambda x: pltpu.with_memory_space_constraint(x, pltpu.HBM)
        f32 = jnp.float32
        flat = jax.ShapeDtypeStruct((1, NPTS), f32)
        table = jax.ShapeDtypeStruct((PXU, PYZ), f32)
        big = lambda *dims: pltpu.VMEM((*dims, LANES), f32)
        small = lambda *dims: pltpu.VMEM((*dims, 128), f32)
        dma = pltpu.SemaphoreType.DMA
        outs = pl.pallas_call(
            functools.partial(step_kernel, events, slices),
            out_shape=(flat, flat, flat, flat, table),
            in_specs=[there] * 7 + [pl.BlockSpec(memory_space=pltpu.SMEM)] + [there] * 2,
            out_specs=(vmem,) * 5,
            scratch_shapes=[
                pltpu.VMEM((4, 1, NPTS), f32),
                pltpu.VMEM((NPTS,), f32),
                small(280),
                small(8),
                small(136),
                small(136),
                pltpu.VMEM((125, 256), f32),
                pltpu.VMEM((8, 256), jnp.int32),
                big(56),
                small(16),
                big(32),
                pltpu.VMEM((2, 624, 256), jnp.bfloat16),
                big(624),
                big(40),
                big(32),
                big(32),
                big(32),
                big(32),
                big(2),
                big(8),
                big(2),
                big(8),
                big(8),
                big(2),
                big(2),
                big(8),
                big(8),
                big(8),
                big(32),
                big(32),
                small(events + 1, 24),
                small(events, 24),
                small(events, 24),
                small(2, 24),
                small(2, 2, 24),
                small(2, 2, 8),
                small(events + 1, 16),
                small(events + 1, 16),
                small(events + 1, 8),
                big(events, 5),
                big(5),
                big(5),
                big(16),
                dma((9,)),
                dma((5,)),
                dma((5,)),
                dma,
                dma,
                dma,
                dma,
                dma((2, 4)),
                dma((2, 4)),
                dma,
                dma,
                dma((events - 1,)),
                pltpu.SemaphoreType.REGULAR,
                dma((2, events)),
                dma,
                dma((2, events)),
                dma,
                dma,
                dma,
                dma((3,)),
                dma,
            ],
            compiler_params=pltpu.CompilerParams(
                collective_id=0, has_side_effects=True, vmem_limit_bytes=40 << 20
            ),
        )(
            *map(stay, (fd, fv, ad, av, inverse_mass, shear, connectivity)),
            count,
            stay(jnp.asarray(lane_tables())),
            stay(jnp.asarray(band_table())),
        )
        fdn, fvn, adn, avn, sk = pl.pallas_call(
            store_kernel,
            out_shape=(flat, flat, flat, flat, table),
            in_specs=[vmem] * 5,
            out_specs=(there,) * 5,
            scratch_shapes=[dma((5,))],
            compiler_params=pltpu.CompilerParams(vmem_limit_bytes=4 << 20),
        )(*outs)
        return fdn, fvn, adn, avn, sk

    return run


def solution(mesh):
    both = P("event", "cuts")
    return jax.shard_map(
        on_device(mesh.shape["event"], mesh.shape["cuts"]),
        mesh=mesh,
        in_specs=(
            both,
            both,
            both,
            both,
            P("cuts"),
            P(None, "cuts"),
            P(None, "cuts"),
            P("cuts", None),
            P("cuts"),
        ),
        out_specs=(both, both, both, both, P("cuts", None)),
        check_vma=False,
    )
```
